32 devices in a mesh: groups: 2 (over y), wide: 4 (over z), heads: 4 (over x, core).
Axes of the slice: x: 2, y: 2, z: 4, core: 2. Of those that a mesh axis runs over, the one named last changes fastest.
Arguments:
- video_hidden: bfloat16 [2048, 4096], P(('groups', 'wide'), 'heads'), parts along dimension 0, may hold values from -6 to 6
- audio_hidden: bfloat16 [512, 2048], P(('groups', 'wide'), 'heads'), parts along dimension 0, may hold values from -6 to 6
- video_query: bfloat16 [2048, 2048], P(('groups', 'wide'), 'heads'), parts along dimension 0, may hold values from -8 to 8
- video_key: bfloat16 [2048, 2048], P(('groups', 'wide'), 'heads'), parts along dimension 0, may hold values from -8 to 8
- video_value: bfloat16 [2048, 2048], P(('groups', 'wide'), 'heads'), parts along dimension 0, may hold values from -6 to 6
- audio_query: bfloat16 [512, 1024], P(('groups', 'wide'), 'heads'), parts along dimension 0, may hold values from -8 to 8
- audio_key: bfloat16 [512, 1024], P(('groups', 'wide'), 'heads'), parts along dimension 0, may hold values from -8 to 8
- audio_value: bfloat16 [512, 1024], P(('groups', 'wide'), 'heads'), parts along dimension 0, may hold values from -6 to 6
- cross_video_query: bfloat16 [2048, 1024], P(('groups', 'wide'), 'heads'), parts along dimension 0, may hold values from -8 to 8
- cross_audio_key: bfloat16 [512, 1024], P(('groups', 'wide'), 'heads'), parts along dimension 0, may hold values from -8 to 8
- cross_audio_value: bfloat16 [512, 1024], P(('groups', 'wide'), 'heads'), parts along dimension 0, may hold values from -6 to 6
- cross_audio_query: bfloat16 [512, 1024], P(('groups', 'wide'), 'heads'), parts along dimension 0, may hold values from -8 to 8
- cross_video_key: bfloat16 [2048, 1024], P(('groups', 'wide'), 'heads'), parts along dimension 0, may hold values from -8 to 8
- cross_video_value: bfloat16 [2048, 1024], P(('groups', 'wide'), 'heads'), parts along dimension 0, may hold values from -6 to 6
- video_self_out: bfloat16 [2048, 4096], P('heads', 'wide'), may hold values from -0.125 to 0.125
- video_cross_out: bfloat16 [1024, 4096], P('heads', 'wide'), may hold values from -0.1875 to 0.1875
- audio_self_out: bfloat16 [1024, 2048], P('heads', 'wide'), may hold values from -0.1875 to 0.1875
- audio_cross_out: bfloat16 [1024, 2048], P('heads', 'wide'), may hold values from -0.1875 to 0.1875
- intersection: int32 [8, 5], P('groups'), parts along dimension 0, may hold values from 0 to 1, as said below
Outputs:
- video_out: bfloat16 [2048, 4096], P(('groups', 'wide'), 'heads'), parts along dimension 0
- audio_out: bfloat16 [512, 2048], P(('groups', 'wide'), 'heads'), parts along dimension 0
The draws below stay inside these ranges and needn't reach their ends.
There are 2 independent parts, one for each index of `groups`. The reference program is written for one: setup_inputs(seed, part) draws one part's arguments, and reference() takes and returns one part's arrays. A program takes and returns all parts, laid end to end along the dimension named above; an argument that names none is the same for every part. Nothing has to cross between parts.
Inputs may be any that keep to these rules, and one draw needn't show every extreme that they name: `intersection`: column 2 is 1 in every row; entries that would pair a block with one outside the clip are ignored.
All inputs are finite; a program needn't handle non-finite values.
Results may differ from the reference program's by a relative error of at most 0.012.
Values may be sent and summed in bfloat16 or wider, within the bound.
No kernel may reach another device: no remote copies, remote signals or barrier semaphores. Data moves between devices by JAX's collectives and lax.ppermute only.
A program may use at most 64 MiB of HBM per device.

```python
import math
import jax
import jax.numpy as jnp
from jax import lax

DV = 4096
DA = 2048
HDV = 128
HDA = 64
HEADS = 16
REACH = 2
TV_DEV = 256
TA_DEV = 64
SPAN = 5
BLOCKS = 4
NV = 1024
NA = 256
N_HEADS = 4


def attention_pair(base_key, query_count, key_count, head_size):
    split_keys = jax.random.split(base_key, 2)
    queries = jnp.clip(3.0 * jax.random.normal(split_keys[0], (query_count, HEADS * head_size), jnp.float32), -8.0, 8.0)
    key_rows = jnp.clip(jax.random.normal(split_keys[1], (key_count, HEADS * head_size), jnp.float32), -4.0, 4.0)
    return (queries, key_rows)


def draw_video_query(key, part):
    return attention_pair(jax.random.fold_in(key, 11), NV, NV, HDV)[0].astype(jnp.bfloat16)


def draw_video_key(key, part):
    return attention_pair(jax.random.fold_in(key, 11), NV, NV, HDV)[1].astype(jnp.bfloat16)


def draw_audio_query(key, part):
    return attention_pair(jax.random.fold_in(key, 12), NA, NA, HDA)[0].astype(jnp.bfloat16)


def draw_audio_key(key, part):
    return attention_pair(jax.random.fold_in(key, 12), NA, NA, HDA)[1].astype(jnp.bfloat16)


def draw_cross_video_query(key, part):
    return attention_pair(jax.random.fold_in(key, 13), NV, NA, HDA)[0].astype(jnp.bfloat16)


def draw_cross_audio_key(key, part):
    return attention_pair(jax.random.fold_in(key, 13), NV, NA, HDA)[1].astype(jnp.bfloat16)


def draw_cross_audio_query(key, part):
    return attention_pair(jax.random.fold_in(key, 14), NA, NV, HDA)[0].astype(jnp.bfloat16)


def draw_cross_video_key(key, part):
    return attention_pair(jax.random.fold_in(key, 14), NA, NV, HDA)[1].astype(jnp.bfloat16)


def draw_intersection(key, part):
    level_key, rolled_key = jax.random.split(jax.random.fold_in(key, 15))
    levels = jax.random.randint(level_key, (BLOCKS, 1), 1, 5)
    rolled = jax.random.randint(rolled_key, (BLOCKS, SPAN), 0, 5)
    intersection_table = (rolled < levels).astype(jnp.int32)
    column = jnp.arange(SPAN, dtype=jnp.int32)
    return jnp.where(column[None, :] == REACH, 1, intersection_table).astype(jnp.int32)


def steps_of(stream_key, extent, cuts, least, top_value):
    gain = 1.0
    for dim, shards_of in cuts:
        draws = jax.random.uniform(jax.random.fold_in(jax.random.fold_in(stream_key, 6), dim), (shards_of,), jnp.float32, least / len(cuts), top_value / len(cuts))
        gain = gain * jnp.repeat(jnp.exp(draws), extent[dim] // shards_of).reshape((-1,) + (1,) * (len(extent) - 1 - dim))
    return gain


def noise(key, shape, spread, bound, cuts=(), held_as=jnp.bfloat16):
    values = spread * jax.random.normal(key, shape, jnp.float32)
    if cuts:
        values = values * steps_of(key, shape, cuts, -0.22, 0.18)
    return jnp.clip(values, -bound, bound).astype(held_as)


def setup_inputs(seed: int = 0, part: int = 0) -> dict:
    splits = jax.random.split(jax.random.key(seed), 20)
    part_keys = jax.random.split(jax.random.fold_in(splits[19], part), 20)
    return {
        "video_hidden": noise(part_keys[0], (NV, DV), 1.0, 6.0, ((0, 4), (1, 4))),
        "audio_hidden": noise(part_keys[1], (NA, DA), 1.0, 6.0, ((0, 4), (1, 4))),
        "video_query": draw_video_query(jax.random.fold_in(jax.random.fold_in(splits[19], part), 71), part),
        "video_key": draw_video_key(jax.random.fold_in(jax.random.fold_in(splits[19], part), 71), part),
        "video_value": noise(part_keys[4], (NV, HEADS * HDV), 1.0, 6.0, ((0, 4), (1, 4))),
        "audio_query": draw_audio_query(jax.random.fold_in(jax.random.fold_in(splits[19], part), 71), part),
        "audio_key": draw_audio_key(jax.random.fold_in(jax.random.fold_in(splits[19], part), 71), part),
        "audio_value": noise(part_keys[7], (NA, HEADS * HDA), 1.0, 6.0, ((0, 4), (1, 4))),
        "cross_video_query": draw_cross_video_query(jax.random.fold_in(jax.random.fold_in(splits[19], part), 71), part),
        "cross_audio_key": draw_cross_audio_key(jax.random.fold_in(jax.random.fold_in(splits[19], part), 71), part),
        "cross_audio_value": noise(part_keys[10], (NA, HEADS * HDA), 1.0, 6.0, ((0, 4), (1, 4))),
        "cross_audio_query": draw_cross_audio_query(jax.random.fold_in(jax.random.fold_in(splits[19], part), 71), part),
        "cross_video_key": draw_cross_video_key(jax.random.fold_in(jax.random.fold_in(splits[19], part), 71), part),
        "cross_video_value": noise(part_keys[13], (NV, HEADS * HDA), 1.0, 6.0, ((0, 4), (1, 4))),
        "video_self_out": noise(splits[14], (HEADS * HDV, DV), (HEADS * HDV) ** -0.5, 0.125, ((0, 4), (1, 4))),
        "video_cross_out": noise(splits[15], (HEADS * HDA, DV), (HEADS * HDA) ** -0.5, 0.1875, ((0, 4), (1, 4))),
        "audio_self_out": noise(splits[16], (HEADS * HDA, DA), (HEADS * HDA) ** -0.5, 0.1875, ((0, 4), (1, 4))),
        "audio_cross_out": noise(splits[17], (HEADS * HDA, DA), (HEADS * HDA) ** -0.5, 0.1875, ((0, 4), (1, 4))),
        "intersection": draw_intersection(jax.random.fold_in(jax.random.fold_in(splits[19], part), 71), part),
    }


def attend(queries, key_rows, value_rows, head_size, allowed):
    row_count = queries.shape[0]
    query_heads = queries.reshape(row_count, HEADS, head_size).transpose(1, 0, 2)
    key_heads = key_rows.reshape(key_rows.shape[0], HEADS, head_size).transpose(1, 0, 2)
    value_heads = value_rows.reshape(value_rows.shape[0], HEADS, head_size).transpose(1, 0, 2)

    def one_head(operands):
        query_one, key_one, value_one = operands
        scores = jnp.dot(query_one, key_one.T, preferred_element_type=jnp.float32) * (1.0 / math.sqrt(head_size))
        if allowed is not None:
            scores = jnp.where(allowed, scores, -1e+30)
        maximum = lax.optimization_barrier(jnp.max(scores, axis=1, keepdims=True))
        weights = jnp.exp(scores - maximum)
        if allowed is not None:
            weights = jnp.where(allowed, weights, 0.0)
        totals = lax.optimization_barrier(jnp.sum(weights, axis=1, keepdims=True))
        mixed = jnp.dot(weights.astype(jnp.bfloat16), value_one, preferred_element_type=jnp.float32)
        return (mixed / totals).astype(jnp.bfloat16)
    result = lax.map(one_head, (query_heads, key_heads, value_heads))
    return result.transpose(1, 0, 2).reshape(row_count, HEADS * head_size)

def cross_mask(intersection):
    video_blocks = jnp.arange(NV, dtype=jnp.int32) // TV_DEV
    audio_blocks = jnp.arange(NA, dtype=jnp.int32) // TA_DEV
    offsets = audio_blocks[None, :] - video_blocks[:, None] + REACH
    inside = (offsets >= 0) & (offsets < SPAN)
    picked = intersection[video_blocks[:, None], jnp.clip(offsets, 0, SPAN - 1)]
    return inside & (picked > 0)

def project(self_part, cross_part, self_weight, cross_weight, self_size, cross_size, hidden):
    per_group = HEADS // N_HEADS
    total = hidden.astype(jnp.float32)
    for head_group in range(N_HEADS):
        self_cols = self_part[:, head_group * per_group * self_size:(head_group + 1) * per_group * self_size]
        cross_cols = cross_part[:, head_group * per_group * cross_size:(head_group + 1) * per_group * cross_size]
        self_rows = self_weight[head_group * per_group * self_size:(head_group + 1) * per_group * self_size]
        cross_rows = cross_weight[head_group * per_group * cross_size:(head_group + 1) * per_group * cross_size]
        partial_value = jnp.dot(self_cols, self_rows, preferred_element_type=jnp.float32) + jnp.dot(cross_cols, cross_rows, preferred_element_type=jnp.float32)
        total = total + lax.optimization_barrier(partial_value.astype(jnp.bfloat16)).astype(jnp.float32)
    return total.astype(jnp.bfloat16)

def reference(video_hidden, audio_hidden, video_query, video_key, video_value, audio_query, audio_key, audio_value, cross_video_query, cross_audio_key, cross_audio_value, cross_audio_query, cross_video_key, cross_video_value, video_self_out, video_cross_out, audio_self_out, audio_cross_out, intersection):
    video_self = attend(video_query, video_key, video_value, HDV, None)
    audio_self = attend(audio_query, audio_key, audio_value, HDA, None)
    allowed = cross_mask(intersection)
    video_cross = attend(cross_video_query, cross_audio_key, cross_audio_value, HDA, allowed)
    audio_cross = attend(cross_audio_query, cross_video_key, cross_video_value, HDA, allowed.T)
    video_out = project(video_self, video_cross, video_self_out, video_cross_out, HDV, HDA, video_hidden)
    audio_out = project(audio_self, audio_cross, audio_self_out, audio_cross_out, HDA, HDA, audio_hidden)
    return (video_out, audio_out)
```

```python
import functools
import math

import jax
import jax.numpy as jnp
from jax import lax
from jax.experimental import pallas as pl
from jax.experimental.pallas import tpu as pltpu
from jax.sharding import PartitionSpec as P

HDV = 128
HDA = 64
REACH = 2


def passed_along(value, axis, by):
    length = lax.axis_size(axis)
    pairs = [(i, i + by) for i in range(length) if 0 <= i + by < length]
    return lax.ppermute(value, axis, pairs)


def empty_state(row_count, head_count, head_size):
    return (
        jnp.full((head_count, row_count), -1e30, jnp.float32),
        jnp.zeros((head_count, row_count), jnp.float32),
        jnp.zeros((head_count, row_count, head_size), jnp.float32),
    )


def absorb(state, queries, key_rows, value_rows, head_size, allowed):
    maxima, totals, running = state
    head_count = queries.shape[1] // head_size
    query_heads = queries.reshape(queries.shape[0], head_count, head_size)
    key_heads = key_rows.reshape(key_rows.shape[0], head_count, head_size)
    value_heads = value_rows.reshape(value_rows.shape[0], head_count, head_size)
    scores = jnp.einsum(
        "qhd,khd->hqk", query_heads, key_heads, preferred_element_type=jnp.float32
    ) * (1.0 / math.sqrt(head_size))
    if allowed is not None:
        scores = jnp.where(allowed[None, None, :], scores, -1e30)
    new_peak = jnp.maximum(maxima, jnp.max(scores, axis=2))
    weights = jnp.exp(scores - new_peak[:, :, None])
    if allowed is not None:
        weights = jnp.where(allowed[None, None, :], weights, 0.0)
    rescale = jnp.exp(maxima - new_peak)
    totals = totals * rescale + jnp.sum(weights, axis=2)
    running = running * rescale[:, :, None] + jnp.einsum(
        "hqk,khd->hqd",
        weights.astype(jnp.bfloat16),
        value_heads,
        preferred_element_type=jnp.float32,
    )
    return (new_peak, totals, running)


def finish(state, head_size):
    maxima, totals, running = state
    result = running / totals[:, :, None]
    return (
        result.transpose(1, 0, 2)
        .reshape(result.shape[1], result.shape[0] * head_size)
        .astype(jnp.bfloat16)
    )


def permitted(key_blocks, position, table_row, wide_count):
    offsets = key_blocks - position + REACH
    matches = (offsets[:, None] == jnp.arange(2 * REACH + 1, dtype=jnp.int32)[None, :]) & (
        table_row[None, :] > 0
    )
    inside = (key_blocks >= 0) & (key_blocks < wide_count)
    return jnp.any(matches, axis=1) & inside


def shards(
    video_hidden,
    audio_hidden,
    video_query,
    video_key,
    video_value,
    audio_query,
    audio_key,
    audio_value,
    cross_video_query,
    cross_audio_key,
    cross_audio_value,
    cross_audio_query,
    cross_video_key,
    cross_video_value,
    video_self_out,
    video_cross_out,
    audio_self_out,
    audio_cross_out,
    intersection,
):
    position = lax.axis_index("wide")
    wide_count = lax.axis_size("wide")
    video_count = video_query.shape[0]
    audio_count = audio_query.shape[0]
    head_count = video_query.shape[1] // HDV
    video_start = empty_state(video_count, head_count, HDV)
    audio_start = empty_state(audio_count, head_count, HDA)
    carried = (video_start, audio_start)
    portion = (
        lax.all_gather(video_key, "wide", axis=0, tiled=True),
        lax.all_gather(video_value, "wide", axis=0, tiled=True),
        lax.all_gather(audio_key, "wide", axis=0, tiled=True),
        lax.all_gather(audio_value, "wide", axis=0, tiled=True),
    )
    video_state = absorb(carried[0], video_query, portion[0], portion[1], HDV, None)
    audio_state = absorb(carried[1], audio_query, portion[2], portion[3], HDA, None)
    table_row = lax.dynamic_slice_in_dim(intersection, position, 1, 0)[0]
    padded_table = jnp.pad(intersection, ((REACH, REACH), (0, 0)))
    flag_row = jnp.diagonal(
        jnp.fliplr(lax.dynamic_slice_in_dim(padded_table, position, 2 * REACH + 1, 0))
    )
    stacked = jnp.concatenate(
        [cross_audio_key, cross_audio_value, cross_video_key, cross_video_value], 0
    )

    def take_cross(carried, portion, block):
        audio_keys = portion[:audio_count]
        audio_values = portion[audio_count : 2 * audio_count]
        video_keys = portion[2 * audio_count : 2 * audio_count + video_count]
        video_values = portion[2 * audio_count + video_count :]
        audio_blocks = jnp.full((audio_count,), block, jnp.int32)
        video_blocks = jnp.full((video_count,), block, jnp.int32)
        return (
            absorb(
                carried[0],
                cross_video_query,
                audio_keys,
                audio_values,
                HDA,
                permitted(audio_blocks, position, table_row, wide_count),
            ),
            absorb(
                carried[1],
                cross_audio_query,
                video_keys,
                video_values,
                HDA,
                permitted(video_blocks, position, flag_row, wide_count),
            ),
        )

    cross_start = (
        empty_state(video_count, head_count, HDA),
        empty_state(audio_count, head_count, HDA),
    )
    carried = take_cross(cross_start, stacked, position)
    for offset in range(-REACH, REACH + 1):
        if offset != 0:
            nearby = passed_along(stacked, "wide", -offset)
            carried = take_cross(carried, nearby, position + offset)
    to_video, to_audio = carried
    video_joined = jnp.concatenate([finish(video_state, HDV), finish(to_video, HDA)], 1)
    audio_joined = jnp.concatenate([finish(audio_state, HDA), finish(to_audio, HDA)], 1)
    video_weights = jnp.concatenate([video_self_out, video_cross_out], 0)
    audio_weights = jnp.concatenate([audio_self_out, audio_cross_out], 0)
    video_terms = jnp.dot(
        video_joined,
        lax.all_gather(video_weights, "wide", axis=1, tiled=True),
        preferred_element_type=jnp.float32,
    )
    audio_terms = jnp.dot(
        audio_joined,
        lax.all_gather(audio_weights, "wide", axis=1, tiled=True),
        preferred_element_type=jnp.float32,
    )
    video_sum, audio_sum = (
        lax.psum_scatter(
            video_terms.astype(jnp.bfloat16), "heads", scatter_dimension=1, tiled=True
        ).astype(jnp.float32),
        lax.psum_scatter(
            audio_terms.astype(jnp.bfloat16), "heads", scatter_dimension=1, tiled=True
        ).astype(jnp.float32),
    )
    video_out = (video_hidden.astype(jnp.float32) + video_sum).astype(jnp.bfloat16)
    audio_out = (audio_hidden.astype(jnp.float32) + audio_sum).astype(jnp.bfloat16)
    return (video_out, audio_out)


def packed_rows(video_count, audio_count):
    return 3 * video_count + video_count + video_count // 2 + 3 * audio_count


def low_half(tile, odd):
    flipped = jnp.concatenate([tile[:, HDA:], tile[:, :HDA]], axis=1)
    return jnp.where(odd, flipped, tile)[:, :HDA]


def pack_kernel(
    position_ref, vq, vk, vv, aq, ak, av, cvq, cak, cav, caq, cvk, cvv, *outs
):
    count = len(outs)
    position = position_ref[0]
    video_count = vq.shape[0]
    audio_count = aq.shape[0]
    for shift in range(count):
        head = lax.rem(position + shift, count)
        wide_at = pl.multiple_of(head * HDV, HDV)
        pair_at = pl.multiple_of((head // 2) * HDV, HDV)
        odd = lax.rem(head, 2) == 1
        out = outs[shift]

        def narrow(ref):
            tile = ref[:, pl.ds(pair_at, HDV)].astype(jnp.float32)
            return low_half(tile, odd)

        def put(row, left, right):
            out[row : row + left.shape[0], :] = jnp.concatenate(
                [left, right], axis=1
            ).astype(jnp.bfloat16)

        row = 0
        for ref in (vq, vk, vv):
            out[row : row + video_count, :] = ref[:, pl.ds(wide_at, HDV)]
            row += video_count
        put(row, narrow(cvq), narrow(cvk))
        row += video_count
        values = narrow(cvv)
        half = video_count // 2
        put(row, values[:half], values[half:])
        row += half
        put(row, narrow(aq), narrow(ak))
        row += audio_count
        put(row, narrow(av), narrow(caq))
        row += audio_count
        put(row, narrow(cak), narrow(cav))


def softmax_mix(scores, values):
    peak = jnp.max(scores, axis=1, keepdims=True)
    weights = jnp.exp(scores - peak)
    totals = jnp.sum(weights, axis=1, keepdims=True)
    mixed = jnp.dot(
        weights.astype(jnp.bfloat16), values, preferred_element_type=jnp.float32
    )
    return mixed / totals


def dot_t(left, right):
    return lax.dot_general(
        left, right, (((1,), (1,)), ((), ())), preferred_element_type=jnp.float32
    )


def attend_kernel(video_count, audio_count, position_ref, table_ref, *refs):
    parts = refs[:-2]
    out, scratch = refs[-2], refs[-1]
    count = len(parts)
    position = position_ref[0]
    blocks = [lax.rem(position + count - shift, count) for shift in range(count)]
    r_cross = 3 * video_count
    r_value = r_cross + video_count
    r_audio = r_value + video_count // 2

    def flag(video_block, audio_block):
        offset = audio_block - video_block + REACH
        inside = (offset >= 0) & (offset <= 2 * REACH)
        entry = table_ref[video_block, jnp.clip(offset, 0, 2 * REACH)]
        return (inside & (entry > 0)).astype(jnp.int32)

    flags = [[flag(b, a) for a in blocks] for b in blocks]

    def masked(scores, row_flags, width):
        block = lax.broadcasted_iota(jnp.int32, (1, scores.shape[1]), 1) // width
        keep = jnp.zeros((1, scores.shape[1]), jnp.int32)
        for i, value in enumerate(row_flags):
            keep = jnp.where(block == i, value, keep)
        return jnp.where(keep > 0, scores, -1e30)

    def rows(start, size):
        return jnp.concatenate([p[start : start + size, :] for p in parts], axis=0)

    cross = rows(r_cross, video_count)
    cross_video_keys = cross[:, HDA:]
    cross_values = jnp.concatenate(
        [
            half
            for p in parts
            for half in (
                p[r_value : r_value + video_count // 2, :HDA],
                p[r_value : r_value + video_count // 2, HDA:],
            )
        ],
        axis=0,
    )
    first = rows(r_audio, audio_count)
    second = rows(r_audio + audio_count, audio_count)
    third = rows(r_audio + 2 * audio_count, audio_count)
    audio_query, audio_key = first[:, :HDA], first[:, HDA:]
    audio_value, cross_audio_query = second[:, :HDA], second[:, HDA:]
    cross_audio_key, cross_audio_value = third[:, :HDA], third[:, HDA:]
    scale = 1.0 / math.sqrt(HDA)
    audio_self = softmax_mix(dot_t(audio_query, audio_key) * scale, audio_value)
    audio_at = count * video_count + count * video_count // 2
    for i in range(count):
        lo, hi = i * audio_count, (i + 1) * audio_count
        scores = dot_t(cross_audio_query[lo:hi], cross_video_keys) * scale
        mixed = softmax_mix(
            masked(scores, [flags[j][i] for j in range(count)], video_count), cross_values
        )
        at = pl.multiple_of(audio_at + blocks[i] * audio_count, audio_count)
        out[pl.ds(at, audio_count), :] = jnp.concatenate(
            [audio_self[lo:hi], mixed], axis=1
        ).astype(jnp.bfloat16)
    for i in range(count):
        queries = parts[i][r_cross : r_cross + video_count, :HDA]
        scores = dot_t(queries, cross_audio_key) * scale
        mixed = softmax_mix(masked(scores, flags[i], audio_count), cross_audio_value)
        scratch[blocks[i]] = mixed
    for pair in range(count // 2):
        at = count * video_count + pair * video_count
        out[at : at + video_count, :] = jnp.concatenate(
            [scratch[2 * pair], scratch[2 * pair + 1]], axis=1
        ).astype(jnp.bfloat16)
    keys = rows(video_count, video_count)
    values = rows(2 * video_count, video_count)
    scale = 1.0 / math.sqrt(HDV)
    for i in range(count):
        scores = dot_t(parts[i][:video_count, :], keys) * scale
        at = pl.multiple_of(blocks[i] * video_count, video_count)
        out[pl.ds(at, video_count), :] = softmax_mix(scores, values).astype(jnp.bfloat16)


def project_kernel(
    video_count, audio_count, place_ref, vs_w, vc_w, as_w, ac_w, *refs
):
    outs, (video_w, audio_w) = refs[-4:-2], refs[-2:]
    parts = refs[:-4]
    count = len(parts)
    position, head_place = place_ref[0], place_ref[1]
    for shift in range(count):
        head = lax.rem(position + count - shift, count)
        video_w[shift * HDV : (shift + 1) * HDV, :] = vs_w[
            pl.ds(pl.multiple_of(head * HDV, HDV), HDV), :
        ]
        small = pl.ds(pl.multiple_of(head * HDA, HDA), HDA)
        base = count * HDV + shift * HDA
        video_w[base : base + HDA, :] = vc_w[small, :]
        audio_w[shift * HDV : shift * HDV + HDA, :] = as_w[small, :]
        audio_w[shift * HDV + HDA : (shift + 1) * HDV, :] = ac_w[small, :]
    piece = video_count // count
    small_piece = audio_count // count
    width = audio_w.shape[1]
    folds = video_w.shape[1] // width
    lane = lax.broadcasted_iota(jnp.int32, (piece, HDV), 1)

    def flip(tile):
        return jnp.concatenate([tile[:, HDA:], tile[:, :HDA]], axis=1)

    for relative in range(count):
        quarter = jnp.bitwise_xor(head_place, relative)
        lines = []
        audio_lines = []
        for block in range(count):
            at = pl.ds(
                pl.multiple_of(block * video_count + quarter * piece, piece), piece
            )
            line = [p[at, :] for p in parts]
            at = pl.ds(
                pl.multiple_of(
                    count * video_count + (block // 2) * video_count + quarter * piece,
                    piece,
                ),
                piece,
            )
            for pair in range(count // 2):
                left = parts[2 * pair][at, :].astype(jnp.float32)
                right = parts[2 * pair + 1][at, :].astype(jnp.float32)
                if block % 2 == 0:
                    right = flip(right)
                else:
                    left = flip(left)
                line.append(jnp.where(lane < HDA, left, right).astype(jnp.bfloat16))
            lines.append(jnp.concatenate(line, axis=1))
            at = pl.ds(
                pl.multiple_of(
                    count * video_count
                    + count * video_count // 2
                    + block * audio_count
                    + quarter * small_piece,
                    small_piece,
                ),
                small_piece,
            )
            audio_lines.append(jnp.concatenate([p[at, :] for p in parts], axis=1))
        video_terms = jnp.dot(
            jnp.concatenate(lines, axis=0), video_w[...], preferred_element_type=jnp.float32
        ).astype(jnp.bfloat16)
        audio_terms = jnp.dot(
            jnp.concatenate(audio_lines, axis=0),
            audio_w[...],
            preferred_element_type=jnp.float32,
        ).astype(jnp.bfloat16)
        out = outs[relative % 2]
        slot = relative // 2
        for block in range(count):
            for fold in range(folds):
                out[slot, block, fold * piece : (fold + 1) * piece, :] = video_terms[
                    block * piece : (block + 1) * piece, fold * width : (fold + 1) * width
                ]
            out[slot, block, folds * piece :, :] = audio_terms[
                block * small_piece : (block + 1) * small_piece, :
            ]


def halve_kernel(kept, arrived, *outs):
    half = kept.shape[0] // 2
    for slot in range(kept.shape[0]):
        total = kept[slot].astype(jnp.float32) + arrived[slot].astype(jnp.float32)
        outs[slot % 2][slot // 2] = total.astype(jnp.bfloat16)


def spread_kernel(place_ref, kept, arrived, *outs):
    count = len(outs)
    for step in range(count):
        block = lax.rem(place_ref[1] + step, count)
        total = kept[0, block].astype(jnp.float32) + arrived[0, block].astype(jnp.float32)
        outs[step][...] = total.astype(jnp.bfloat16)


def finish_kernel(place_ref, video_hidden, audio_hidden, *refs):
    parts, (video_out, audio_out) = refs[:-2], refs[-2:]
    count = len(parts)
    piece = video_hidden.shape[0] // count
    small_piece = audio_hidden.shape[0] // count
    width = audio_hidden.shape[1]
    folds = video_hidden.shape[1] // width
    for step in range(count):
        quarter = lax.rem(place_ref[0] + count - step, count)
        at = pl.ds(pl.multiple_of(quarter * piece, piece), piece)
        for fold in range(folds):
            lanes = slice(fold * width, (fold + 1) * width)
            video_out[at, lanes] = (
                video_hidden[at, lanes].astype(jnp.float32)
                + parts[step][fold * piece : (fold + 1) * piece, :].astype(jnp.float32)
            ).astype(jnp.bfloat16)
        at = pl.ds(pl.multiple_of(quarter * small_piece, small_piece), small_piece)
        audio_out[at, :] = (
            audio_hidden[at, :].astype(jnp.float32)
            + parts[step][folds * piece :, :].astype(jnp.float32)
        ).astype(jnp.bfloat16)


VMEM = pl.BlockSpec(memory_space=pltpu.VMEM)
SMEM = pl.BlockSpec(memory_space=pltpu.SMEM)


def whole_call(kernel, scalars, arrays, out_shapes, scratch=()):
    return pl.pallas_call(
        kernel,
        in_specs=[SMEM] * len(scalars) + [VMEM] * len(arrays),
        out_specs=[VMEM] * len(out_shapes),
        out_shape=[jax.ShapeDtypeStruct(s, jnp.bfloat16) for s in out_shapes],
        scratch_shapes=list(scratch),
    )(*scalars, *arrays)


def regrouped(
    video_hidden,
    audio_hidden,
    video_query,
    video_key,
    video_value,
    audio_query,
    audio_key,
    audio_value,
    cross_video_query,
    cross_audio_key,
    cross_audio_value,
    cross_audio_query,
    cross_video_key,
    cross_video_value,
    video_self_out,
    video_cross_out,
    audio_self_out,
    audio_cross_out,
    intersection,
):
    count = lax.axis_size("wide")
    position = lax.axis_index("wide").astype(jnp.int32)
    head_place = lax.axis_index("heads").astype(jnp.int32)
    place = jnp.stack([position, head_place])
    video_count = video_query.shape[0]
    audio_count = audio_query.shape[0]
    rows = packed_rows(video_count, audio_count)
    packed = whole_call(
        pack_kernel,
        (place,),
        (
            video_query,
            video_key,
            video_value,
            audio_query,
            audio_key,
            audio_value,
            cross_video_query,
            cross_audio_key,
            cross_audio_value,
            cross_audio_query,
            cross_video_key,
            cross_video_value,
        ),
        [(rows, HDV)] * count,
    )

    def shifted(value, by):
        return lax.ppermute(value, "wide", [(i, (i + by) % count) for i in range(count)])

    arrived = [packed[0]] + [shifted(packed[s], s) for s in range(1, count)]
    mixed_rows = count * (video_count + video_count // 2 + audio_count)
    (mixed,) = whole_call(
        functools.partial(attend_kernel, video_count, audio_count),
        (place, intersection),
        arrived,
        [(mixed_rows, HDV)],
        (pltpu.VMEM((count, video_count, HDA), jnp.float32),),
    )
    gathered = [mixed] + [shifted(mixed, s) for s in range(1, count)]
    width = audio_self_out.shape[1]
    folds = video_self_out.shape[1] // width
    height = (video_count * folds + audio_count) // count
    kept, leaving = whole_call(
        functools.partial(project_kernel, video_count, audio_count),
        (place,),
        (video_self_out, video_cross_out, audio_self_out, audio_cross_out, *gathered),
        [(count // 2, count, height, width)] * 2,
        (
            pltpu.VMEM((count * (HDV + HDA), video_self_out.shape[1]), jnp.bfloat16),
            pltpu.VMEM((count * 2 * HDA, width), jnp.bfloat16),
        ),
    )
    bit = 1
    while bit < count:
        nearby = lax.ppermute(leaving, "heads", [(i, i ^ bit) for i in range(count)])
        bit *= 2
        if bit < count:
            slots = kept.shape[0] // 2
            kept, leaving = whole_call(
                halve_kernel, (), (kept, nearby), [(slots, count, height, width)] * 2
            )
    pieces = whole_call(spread_kernel, (place,), (kept, nearby), [(height, width)] * count)
    landed = [
        lax.ppermute(
            pieces[step],
            ("wide", "heads"),
            [
                (w * count + h, ((h + step) % count) * count + w)
                for w in range(count)
                for h in range(count)
            ],
        )
        for step in range(count)
    ]
    return tuple(
        whole_call(
            finish_kernel,
            (place,),
            (video_hidden, audio_hidden, *landed),
            [video_hidden.shape, audio_hidden.shape],
        )
    )


def dispatch(*operands):
    count = lax.axis_size("wide")
    head_count = operands[2].shape[1] // HDV
    whole = head_count == count == lax.axis_size("heads")
    if whole and count & (count - 1) == 0 and operands[5].shape[0] % (16 * count) == 0:
        return regrouped(*operands)
    return shards(*operands)


def solution(mesh):
    placed = (
        P(("groups", "wide"), "heads"),
        P(("groups", "wide"), "heads"),
        P(("groups", "wide"), "heads"),
        P(("groups", "wide"), "heads"),
        P(("groups", "wide"), "heads"),
        P(("groups", "wide"), "heads"),
        P(("groups", "wide"), "heads"),
        P(("groups", "wide"), "heads"),
        P(("groups", "wide"), "heads"),
        P(("groups", "wide"), "heads"),
        P(("groups", "wide"), "heads"),
        P(("groups", "wide"), "heads"),
        P(("groups", "wide"), "heads"),
        P(("groups", "wide"), "heads"),
        P("heads", "wide"),
        P("heads", "wide"),
        P("heads", "wide"),
        P("heads", "wide"),
        P("groups", None),
    )
    return jax.shard_map(
        dispatch,
        mesh=mesh,
        in_specs=placed,
        out_specs=(P(("groups", "wide"), "heads"), P(("groups", "wide"), "heads")),
        check_vma=False,
    )
```

```python
import functools
import math

import jax
import jax.numpy as jnp
from jax import lax
from jax.experimental import pallas as pl
from jax.experimental.pallas import tpu as pltpu
from jax.sharding import PartitionSpec as P

HDV = 128
HDA = 64
REACH = 2


def passed_along(value, axis, by):
    length = lax.axis_size(axis)
    pairs = [(i, i + by) for i in range(length) if 0 <= i + by < length]
    return lax.ppermute(value, axis, pairs)


def empty_state(row_count, head_count, head_size):
    return (
        jnp.full((head_count, row_count), -1e30, jnp.float32),
        jnp.zeros((head_count, row_count), jnp.float32),
        jnp.zeros((head_count, row_count, head_size), jnp.float32),
    )


def absorb(state, queries, key_rows, value_rows, head_size, allowed):
    maxima, totals, running = state
    head_count = queries.shape[1] // head_size
    query_heads = queries.reshape(queries.shape[0], head_count, head_size)
    key_heads = key_rows.reshape(key_rows.shape[0], head_count, head_size)
    value_heads = value_rows.reshape(value_rows.shape[0], head_count, head_size)
    scores = jnp.einsum(
        "qhd,khd->hqk", query_heads, key_heads, preferred_element_type=jnp.float32
    ) * (1.0 / math.sqrt(head_size))
    if allowed is not None:
        scores = jnp.where(allowed[None, None, :], scores, -1e30)
    new_peak = jnp.maximum(maxima, jnp.max(scores, axis=2))
    weights = jnp.exp(scores - new_peak[:, :, None])
    if allowed is not None:
        weights = jnp.where(allowed[None, None, :], weights, 0.0)
    rescale = jnp.exp(maxima - new_peak)
    totals = totals * rescale + jnp.sum(weights, axis=2)
    running = running * rescale[:, :, None] + jnp.einsum(
        "hqk,khd->hqd",
        weights.astype(jnp.bfloat16),
        value_heads,
        preferred_element_type=jnp.float32,
    )
    return (new_peak, totals, running)


def finish(state, head_size):
    _, totals, running = state
    result = running / totals[:, :, None]
    return (
        result.transpose(1, 0, 2)
        .reshape(result.shape[1], result.shape[0] * head_size)
        .astype(jnp.bfloat16)
    )


def permitted(key_blocks, position, table_row, wide_count):
    offsets = key_blocks - position + REACH
    matches = (offsets[:, None] == jnp.arange(2 * REACH + 1, dtype=jnp.int32)[None, :]) & (
        table_row[None, :] > 0
    )
    inside = (key_blocks >= 0) & (key_blocks < wide_count)
    return jnp.any(matches, axis=1) & inside


def shards(
    video_hidden,
    audio_hidden,
    video_query,
    video_key,
    video_value,
    audio_query,
    audio_key,
    audio_value,
    cross_video_query,
    cross_audio_key,
    cross_audio_value,
    cross_audio_query,
    cross_video_key,
    cross_video_value,
    video_self_out,
    video_cross_out,
    audio_self_out,
    audio_cross_out,
    intersection,
):
    position = lax.axis_index("wide")
    wide_count = lax.axis_size("wide")
    video_count = video_query.shape[0]
    audio_count = audio_query.shape[0]
    head_count = video_query.shape[1] // HDV
    video_start = empty_state(video_count, head_count, HDV)
    audio_start = empty_state(audio_count, head_count, HDA)
    carried = (video_start, audio_start)
    portion = (
        lax.all_gather(video_key, "wide", axis=0, tiled=True),
        lax.all_gather(video_value, "wide", axis=0, tiled=True),
        lax.all_gather(audio_key, "wide", axis=0, tiled=True),
        lax.all_gather(audio_value, "wide", axis=0, tiled=True),
    )
    video_state = absorb(carried[0], video_query, portion[0], portion[1], HDV, None)
    audio_state = absorb(carried[1], audio_query, portion[2], portion[3], HDA, None)
    table_row = lax.dynamic_slice_in_dim(intersection, position, 1, 0)[0]
    padded_table = jnp.pad(intersection, ((REACH, REACH), (0, 0)))
    flag_row = jnp.diagonal(
        jnp.fliplr(lax.dynamic_slice_in_dim(padded_table, position, 2 * REACH + 1, 0))
    )
    stacked = jnp.concatenate(
        [cross_audio_key, cross_audio_value, cross_video_key, cross_video_value], 0
    )

    def take_cross(carried, portion, block):
        audio_keys = portion[:audio_count]
        audio_values = portion[audio_count : 2 * audio_count]
        video_keys = portion[2 * audio_count : 2 * audio_count + video_count]
        video_values = portion[2 * audio_count + video_count :]
        audio_blocks = jnp.full((audio_count,), block, jnp.int32)
        video_blocks = jnp.full((video_count,), block, jnp.int32)
        return (
            absorb(
                carried[0],
                cross_video_query,
                audio_keys,
                audio_values,
                HDA,
                permitted(audio_blocks, position, table_row, wide_count),
            ),
            absorb(
                carried[1],
                cross_audio_query,
                video_keys,
                video_values,
                HDA,
                permitted(video_blocks, position, flag_row, wide_count),
            ),
        )

    cross_start = (
        empty_state(video_count, head_count, HDA),
        empty_state(audio_count, head_count, HDA),
    )
    carried = take_cross(cross_start, stacked, position)
    for offset in range(-REACH, REACH + 1):
        if offset != 0:
            nearby = passed_along(stacked, "wide", -offset)
            carried = take_cross(carried, nearby, position + offset)
    to_video, to_audio = carried
    video_joined = jnp.concatenate([finish(video_state, HDV), finish(to_video, HDA)], 1)
    audio_joined = jnp.concatenate([finish(audio_state, HDA), finish(to_audio, HDA)], 1)
    video_weights = jnp.concatenate([video_self_out, video_cross_out], 0)
    audio_weights = jnp.concatenate([audio_self_out, audio_cross_out], 0)
    video_terms = jnp.dot(
        video_joined,
        lax.all_gather(video_weights, "wide", axis=1, tiled=True),
        preferred_element_type=jnp.float32,
    )
    audio_terms = jnp.dot(
        audio_joined,
        lax.all_gather(audio_weights, "wide", axis=1, tiled=True),
        preferred_element_type=jnp.float32,
    )
    video_sum, audio_sum = (
        lax.psum_scatter(
            video_terms.astype(jnp.bfloat16), "heads", scatter_dimension=1, tiled=True
        ).astype(jnp.float32),
        lax.psum_scatter(
            audio_terms.astype(jnp.bfloat16), "heads", scatter_dimension=1, tiled=True
        ).astype(jnp.float32),
    )
    video_out = (video_hidden.astype(jnp.float32) + video_sum).astype(jnp.bfloat16)
    audio_out = (audio_hidden.astype(jnp.float32) + audio_sum).astype(jnp.bfloat16)
    return (video_out, audio_out)


VMEM = pl.BlockSpec(memory_space=pltpu.VMEM)
SMEM = pl.BlockSpec(memory_space=pltpu.SMEM)
HBM = pl.BlockSpec(memory_space=pltpu.HBM)
KERNEL_BYTES = 24 * 1024 * 1024


def kernel_call(kernel, scalars, arrays, out_shapes, scratch=(), spaces=None, final=False, held_as=jnp.bfloat16):
    spaces = spaces or [pltpu.VMEM] * len(arrays)
    specs = {pltpu.VMEM: VMEM, pltpu.HBM: HBM}
    out_space = pltpu.HBM if final else pltpu.VMEM
    call = pl.pallas_call(
        kernel,
        in_specs=[SMEM] * len(scalars)
        + [VMEM if s is None else specs[s] for s in spaces],
        out_specs=[VMEM] * len(out_shapes),
        out_shape=[out_space(s, held_as) for s in out_shapes],
        scratch_shapes=list(scratch),
        compiler_params=pltpu.CompilerParams(vmem_limit_bytes=KERNEL_BYTES),
    )
    arrays = [
        pltpu.with_memory_space_constraint(a, pltpu.HBM if s is None else s)
        for a, s in zip(arrays, spaces)
    ]
    return call(*scalars, *arrays)


def flip(tile):
    return jnp.concatenate([tile[:, HDA:], tile[:, :HDA]], axis=1)


def pack_wide_kernel(place_ref, *refs):
    sems = refs[-1]
    sources, outs = refs[:3], refs[3:-1]
    count = len(outs)
    rows = sources[0].shape[0]
    copies = []
    for shift in range(count):
        head = lax.rem(place_ref[0] + shift, count)
        lanes = pl.ds(pl.multiple_of(head * HDV, HDV), HDV)
        for i, source in enumerate(sources):
            copies.append(
                pltpu.make_async_copy(
                    source.at[:, lanes],
                    outs[shift].at[pl.ds(i * rows, rows), :],
                    sems.at[shift * len(sources) + i],
                )
            )
    for copy in copies:
        copy.start()
    for copy in copies:
        copy.wait()


def pack_narrow_kernel(place_ref, aq, ak, av, cvq, cak, cav, caq, cvk, cvv, *outs):
    count = len(outs)
    video_count = cvq.shape[0]
    audio_count = aq.shape[0]
    half = video_count // 2
    for shift in range(count):
        head = lax.rem(place_ref[0] + shift, count)
        lanes = pl.ds(pl.multiple_of((head // 2) * HDV, HDV), HDV)
        odd = lax.rem(head, 2) == 1
        out = outs[shift]
        lane = lax.broadcasted_iota(jnp.int32, (1, HDV), 1)

        def put(row, left, right):
            left, right = left.astype(jnp.float32), right.astype(jnp.float32)
            left = jnp.where(odd, flip(left), left)
            right = jnp.where(odd, right, flip(right))
            out[row : row + left.shape[0], :] = jnp.where(lane < HDA, left, right).astype(
                jnp.bfloat16
            )

        row = 0
        put(row, cvq[:, lanes], cvk[:, lanes])
        row += video_count
        put(row, cvv[:half, lanes], cvv[half:, lanes])
        row += half
        for left, right in ((aq, ak), (av, caq), (cak, cav)):
            put(row, left[:, lanes], right[:, lanes])
            row += audio_count


def softmax_mix(scores, values):
    peak = jnp.max(scores, axis=1, keepdims=True)
    weights = jnp.exp(scores - peak)
    totals = jnp.sum(weights, axis=1, keepdims=True)
    mixed = jnp.dot(
        weights.astype(jnp.bfloat16), values, preferred_element_type=jnp.float32
    )
    return mixed / totals


def dot_t(left, right):
    return lax.dot_general(
        left, right, (((1,), (1,)), ((), ())), preferred_element_type=jnp.float32
    )


def attend_wide_kernel(place_ref, head_ref, *refs):
    parts, outs, sorted_rows = refs[:-3], refs[-3:-1], refs[-1]
    count = len(parts)
    rows = parts[0].shape[0] // 3
    side = rows // (2 * CHUNKS)
    keys = jnp.concatenate([p[rows : 2 * rows, :] for p in parts], axis=0)
    values = jnp.concatenate([p[2 * rows :, :] for p in parts], axis=0)
    scale = 1.0 / math.sqrt(HDV)
    for shift in range(count):
        block = lax.rem(place_ref[0] + count - shift, count)
        scores = dot_t(parts[shift][:rows, :], keys) * scale
        mixed = softmax_mix(scores, values).astype(jnp.bfloat16)
        for half in range(2):
            far, near = owner_of(block, half, head_ref[0], count)
            for c in range(CHUNKS):
                row = (2 * c + half) * side
                sorted_rows[far, c, near, half] = mixed[row : row + side]
    for far in range(2):
        outs[far][...] = sorted_rows[far].reshape(outs[far].shape)


def owner_of(block, half, head_place, count):
    owner = jnp.bitwise_xor(block, half * (count // 2))
    apart = jnp.bitwise_xor(owner, head_place)
    return apart // 2, lax.rem(apart, 2)


def attend_narrow_kernel(video_count, audio_count, place_ref, head_ref, table_ref, *refs):
    parts, outs, (sorted_video, sorted_audio) = refs[:-4], refs[-4:-2], refs[-2:]
    count = len(parts)
    blocks = [lax.rem(place_ref[0] + count - shift, count) for shift in range(count)]
    half = video_count // 2
    r_value = video_count
    r_audio = r_value + half

    def flag(video_block, audio_block):
        offset = audio_block - video_block + REACH
        inside = (offset >= 0) & (offset <= 2 * REACH)
        entry = table_ref[video_block, jnp.clip(offset, 0, 2 * REACH)]
        return (inside & (entry > 0)).astype(jnp.int32)

    flags = [[flag(b, a) for a in blocks] for b in blocks]

    def masked(scores, row_flags, width):
        block = lax.broadcasted_iota(jnp.int32, (1, scores.shape[1]), 1) // width
        keep = jnp.zeros((1, scores.shape[1]), jnp.int32)
        for i, value in enumerate(row_flags):
            keep = jnp.where(block == i, value, keep)
        return jnp.where(keep > 0, scores, -1e30)

    def rows(start, size):
        return jnp.concatenate([p[start : start + size, :] for p in parts], axis=0)

    first = rows(r_audio, audio_count)
    second = rows(r_audio + audio_count, audio_count)
    third = rows(r_audio + 2 * audio_count, audio_count)
    scale = 1.0 / math.sqrt(HDA)
    cross_audio_key, cross_audio_value = third[:, :HDA], third[:, HDA:]
    side = video_count // (2 * CHUNKS)
    small = audio_count // 2
    for i in range(count):
        scores = dot_t(parts[i][:video_count, :HDA], cross_audio_key) * scale
        mixed = softmax_mix(masked(scores, flags[i], audio_count), cross_audio_value)
        for half in range(2):
            far, near = owner_of(blocks[i], half, head_ref[0], count)
            for c in range(CHUNKS):
                row = (2 * c + half) * side
                sorted_video[far, c, near, :, half * HDA : (half + 1) * HDA] = mixed[
                    row : row + side
                ]
    audio_self = softmax_mix(
        dot_t(first[:, :HDA], first[:, HDA:]) * scale, second[:, :HDA]
    )
    queries = second[:, HDA:]
    keys = jnp.concatenate([p[:video_count, HDA:] for p in parts], axis=0)
    values = jnp.concatenate(
        [
            rows_of
            for p in parts
            for rows_of in (p[r_value:r_audio, :HDA], p[r_value:r_audio, HDA:])
        ],
        axis=0,
    )
    for i in range(count):
        lo, hi = i * audio_count, (i + 1) * audio_count
        scores = dot_t(queries[lo:hi], keys) * scale
        mixed = softmax_mix(
            masked(scores, [flags[j][i] for j in range(count)], video_count), values
        )
        both = jnp.concatenate([audio_self[lo:hi], mixed], axis=1)
        for half in range(2):
            far, near = owner_of(blocks[i], half, head_ref[0], count)
            sorted_audio[far, near, half] = both[half * small : (half + 1) * small]
    video_rows = 2 * CHUNKS * side
    for far in range(2):
        outs[far][:video_rows, :] = (
            sorted_video[far].reshape(video_rows, HDV).astype(jnp.bfloat16)
        )
        outs[far][video_rows:, :] = (
            sorted_audio[far].reshape(4 * small, HDV).astype(jnp.bfloat16)
        )


def join_kernel(first, second, out):
    rows = first.shape[0]
    out[:rows, :] = first[...]
    out[rows:, :] = second[...]


def order_kernel(place_ref, vs_w, vc_w, as_w, ac_w, first_w, second_w, cross_w, audio_w):
    count = vs_w.shape[0] // HDV
    for shift in range(count):
        head = lax.rem(place_ref[0] + count - shift, count)
        wide = pl.ds(pl.multiple_of(head * HDV, HDV), HDV)
        small = pl.ds(pl.multiple_of(head * HDA, HDA), HDA)
        at = (shift % (count // 2)) * HDV
        (first_w, second_w)[shift // (count // 2)][at : at + HDV, :] = vs_w[wide, :]
        cross_w[shift * HDA : (shift + 1) * HDA, :] = vc_w[small, :]
        audio_w[shift * HDV : shift * HDV + HDA, :] = as_w[small, :]
        audio_w[shift * HDV + HDA : (shift + 1) * HDV, :] = ac_w[small, :]


def read_slots(slots, position, rows):
    count = (len(slots) + 1) // 2
    found = [slots[0][rows, :]]
    for shift in range(1, count):
        before, after = slots[shift], slots[count - 1 + shift]
        found.append(jnp.where(position >= shift, before[rows, :], after[rows, :]))
    return found


def project_wide_kernel(place_ref, own_first, own_second, far_first, far_second, *refs):
    slots, out = refs[:-1], refs[-1]
    rows = slots[0].shape[0] // 2
    total = 0.0
    for far, pair in enumerate(((own_first, own_second), (far_first, far_second))):
        found = read_slots(slots, place_ref[0], slice(far * rows, (far + 1) * rows))
        for i, weights in enumerate(pair):
            wide = jnp.concatenate(found[2 * i : 2 * i + 2], axis=1)
            total = total + jnp.dot(
                wide, weights[...], preferred_element_type=jnp.float32
            )
    out[...] = total


def project_narrow_kernel(place_ref, own_w, far_w, own_audio_w, far_audio_w, begun, *refs):
    slots, outs = refs[:-2], refs[-2:]
    count = (len(slots) + 1) // 2
    width = own_audio_w.shape[1]
    folds = own_w.shape[1] // width
    side = begun.shape[0] // (4 * CHUNKS)
    video_rows = 2 * CHUNKS * side
    rows = slots[0].shape[0] // 2
    small = (rows - video_rows) // 4
    position = place_ref[0]
    lane = lax.broadcasted_iota(jnp.int32, (1, HDV), 1)
    total = begun[...]
    audio_total = 0.0
    for far in range(2):
        weights, audio_weights = ((own_w, own_audio_w), (far_w, far_audio_w))[far]
        found = [
            t.astype(jnp.float32)
            for t in read_slots(slots, position, slice(far * rows, far * rows + video_rows))
        ]
        flipped = [flip(t) for t in found]
        halves = [
            jnp.concatenate(
                [
                    jnp.where(
                        lane < HDA,
                        (flipped if half else found)[pair],
                        (found if half else flipped)[pair + 1],
                    ).astype(jnp.bfloat16)
                    for pair in range(0, count, 2)
                ],
                axis=1,
            )
            for half in range(2)
        ]
        lines = [
            halves[half][i * side : (i + 1) * side]
            for i in range(2 * CHUNKS)
            for half in range(2)
        ]
        total = total + jnp.dot(
            jnp.concatenate(lines, axis=0),
            weights[...],
            preferred_element_type=jnp.float32,
        )
        found = read_slots(slots, position, slice(far * rows + video_rows, (far + 1) * rows))
        audio_total = audio_total + jnp.dot(
            jnp.concatenate(found, axis=1), audio_weights[...], preferred_element_type=jnp.float32
        )
    total = total.astype(jnp.bfloat16)
    audio_total = audio_total.astype(jnp.bfloat16)
    for near in range(2):
        for half in range(2):
            for c in range(CHUNKS):
                row = ((2 * c + near) * 2 + half) * side
                for fold in range(folds):
                    at = (c * folds + fold) * side
                    outs[near][half, at : at + side, :] = total[
                        row : row + side, fold * width : (fold + 1) * width
                    ]
            row = (near * 2 + half) * small
            outs[near][half, CHUNKS * folds * side :, :] = audio_total[row : row + small]


def settle_kernel(kept, arrived, *outs):
    for half in range(2):
        total = kept[half].astype(jnp.float32) + arrived[half].astype(jnp.float32)
        outs[half][...] = total.astype(jnp.bfloat16)


def finish_kernel(video_hidden, audio_hidden, *refs):
    parts, (video_out, audio_out) = refs[:-2], refs[-2:]
    side = video_hidden.shape[0] // (2 * CHUNKS)
    small = audio_hidden.shape[0] // 2
    width = audio_hidden.shape[1]
    folds = video_hidden.shape[1] // width
    for half, part in enumerate(parts):
        for c in range(CHUNKS):
            row = (2 * c + half) * side
            rows = slice(row, row + side)
            for fold in range(folds):
                lanes = slice(fold * width, (fold + 1) * width)
                at = (c * folds + fold) * side
                video_out[rows, lanes] = (
                    video_hidden[rows, lanes].astype(jnp.float32)
                    + part[at : at + side, :].astype(jnp.float32)
                ).astype(jnp.bfloat16)
        rows = slice(half * small, (half + 1) * small)
        audio_out[rows, :] = (
            audio_hidden[rows, :].astype(jnp.float32)
            + part[CHUNKS * folds * side :, :].astype(jnp.float32)
        ).astype(jnp.bfloat16)


CHUNKS = 1
DIRECT = (False, True)


def exchanged(pieces):
    count = len(pieces)
    return [pieces[0]] + [
        lax.ppermute(pieces[s], "wide", [(i, (i + s) % count) for i in range(count)])
        for s in range(1, count)
    ]


def shared_along(value, direct):
    count = lax.axis_size("wide")
    if direct:
        rest = exchanged([value] * count)[1:]
        return [value] + rest + rest
    before, after = {}, {}
    for far in range(1, count):
        hop = far if far <= 2 else 1
        up = [(i, i + hop) for i in range(count) if 0 <= i + hop - far and i + hop < count]
        down = [(i, i - hop) for i in range(count) if i - hop + far < count and i - hop >= 0]
        source_up = value if far <= 2 else before[far - 1]
        source_down = value if far <= 2 else after[far - 1]
        if 2 * far >= count and source_up is source_down:
            before[far] = after[far] = lax.ppermute(source_up, "wide", up + down)
        else:
            before[far] = lax.ppermute(source_up, "wide", up)
            after[far] = lax.ppermute(source_down, "wide", down)
    return (
        [value]
        + [before[s] for s in range(1, count)]
        + [after[count - s] for s in range(1, count)]
    )


def regrouped(
    video_hidden,
    audio_hidden,
    video_query,
    video_key,
    video_value,
    audio_query,
    audio_key,
    audio_value,
    cross_video_query,
    cross_audio_key,
    cross_audio_value,
    cross_audio_query,
    cross_video_key,
    cross_video_value,
    video_self_out,
    video_cross_out,
    audio_self_out,
    audio_cross_out,
    intersection,
):
    count = lax.axis_size("wide")
    place = lax.axis_index("wide").astype(jnp.int32).reshape(1)
    head_place = lax.axis_index("heads").astype(jnp.int32).reshape(1)
    video_count = video_query.shape[0]
    audio_count = audio_query.shape[0]
    wide = kernel_call(
        pack_wide_kernel,
        (place,),
        (video_query, video_key, video_value),
        [(3 * video_count, HDV)] * count,
        (pltpu.SemaphoreType.DMA((3 * count,)),),
        [pltpu.HBM] * 3,
    )
    wide = exchanged(wide)
    narrow = kernel_call(
        pack_narrow_kernel,
        (place,),
        (
            audio_query,
            audio_key,
            audio_value,
            cross_video_query,
            cross_audio_key,
            cross_audio_value,
            cross_audio_query,
            cross_video_key,
            cross_video_value,
        ),
        [(video_count + video_count // 2 + 3 * audio_count, HDV)] * count,
        spaces=[None] * 9,
    )
    narrow = exchanged(narrow)
    width = audio_self_out.shape[1]
    folds = video_self_out.shape[1] // width

    def across(value, bit):
        return lax.ppermute(value, "heads", [(i, i ^ bit) for i in range(count)])

    half_rows = count // 2 * HDV
    weights = kernel_call(
        order_kernel,
        (place,),
        (video_self_out, video_cross_out, audio_self_out, audio_cross_out),
        [(half_rows, folds * width)] * 2
        + [(count * HDA, folds * width), (count * 2 * HDA, width)],
        spaces=[None] * 4,
    )
    far_weights = [across(value, 2) for value in weights]
    side = video_count // (2 * CHUNKS)
    mine = count * video_count // 2
    near, far = kernel_call(
        attend_wide_kernel,
        (place, head_place),
        wide,
        [(mine, HDV)] * 2,
        (pltpu.VMEM((2, CHUNKS, 2, 2, side, HDV), jnp.bfloat16),),
    )
    far = across(far, 2)
    (message,) = kernel_call(join_kernel, (), (near, far), [(2 * mine, HDV)])
    wide_slots = shared_along(message, DIRECT[0])
    small = audio_count // 2
    rows = 2 * CHUNKS * side + 4 * small
    near, far = kernel_call(
        functools.partial(attend_narrow_kernel, video_count, audio_count),
        (place, head_place, intersection),
        narrow,
        [(rows, HDV)] * 2,
        (
            pltpu.VMEM((2, CHUNKS, 2, side, HDV), jnp.float32),
            pltpu.VMEM((2, 2, 2, small, HDV), jnp.float32),
        ),
    )
    far = across(far, 2)
    (message,) = kernel_call(join_kernel, (), (near, far), [(2 * rows, HDV)])
    narrow_slots = shared_along(message, DIRECT[1])
    (begun,) = kernel_call(
        project_wide_kernel,
        (place,),
        (*weights[:2], *far_weights[:2], *wide_slots),
        [(mine, folds * width)],
        held_as=jnp.float32,
    )
    height = (video_count * folds + audio_count) // 2
    kept, leaving = kernel_call(
        project_narrow_kernel,
        (place,),
        (weights[2], far_weights[2], weights[3], far_weights[3], begun, *narrow_slots),
        [(2, height, width)] * 2,
    )
    halves = kernel_call(settle_kernel, (), (kept, across(leaving, 1)), [(height, width)] * 2)
    landed = [
        lax.ppermute(
            halves[half],
            ("wide", "heads"),
            [
                (w * count + h, (h ^ (half * (count // 2))) * count + w)
                for w in range(count)
                for h in range(count)
            ],
        )
        for half in range(2)
    ]
    return tuple(
        kernel_call(
            finish_kernel,
            (),
            (video_hidden, audio_hidden, *landed),
            [video_hidden.shape, audio_hidden.shape],
            final=True,
        )
    )


def dispatch(*operands):
    count = lax.axis_size("wide")
    head_count = operands[2].shape[1] // HDV
    whole = head_count == count == lax.axis_size("heads")
    if whole and count == 4 and operands[5].shape[0] % (16 * count) == 0:
        return regrouped(*operands)
    return shards(*operands)


def solution(mesh):
    placed = (
        P(("groups", "wide"), "heads"),
        P(("groups", "wide"), "heads"),
        P(("groups", "wide"), "heads"),
        P(("groups", "wide"), "heads"),
        P(("groups", "wide"), "heads"),
        P(("groups", "wide"), "heads"),
        P(("groups", "wide"), "heads"),
        P(("groups", "wide"), "heads"),
        P(("groups", "wide"), "heads"),
        P(("groups", "wide"), "heads"),
        P(("groups", "wide"), "heads"),
        P(("groups", "wide"), "heads"),
        P(("groups", "wide"), "heads"),
        P(("groups", "wide"), "heads"),
        P("heads", "wide"),
        P("heads", "wide"),
        P("heads", "wide"),
        P("heads", "wide"),
        P("groups", None),
    )
    return jax.shard_map(
        dispatch,
        mesh=mesh,
        in_specs=placed,
        out_specs=(P(("groups", "wide"), "heads"), P(("groups", "wide"), "heads")),
        check_vma=False,
    )
```

```python
import functools
import math

import jax
import jax.numpy as jnp
from jax import lax
from jax.experimental import pallas as pl
from jax.experimental.pallas import tpu as pltpu
from jax.sharding import PartitionSpec as P

HDV = 128
HDA = 64
REACH = 2


def passed_along(value, axis, by):
    length = lax.axis_size(axis)
    pairs = [(i, i + by) for i in range(length) if 0 <= i + by < length]
    return lax.ppermute(value, axis, pairs)


def empty_state(row_count, head_count, head_size):
    return (
        jnp.full((head_count, row_count), -1e30, jnp.float32),
        jnp.zeros((head_count, row_count), jnp.float32),
        jnp.zeros((head_count, row_count, head_size), jnp.float32),
    )


def absorb(state, queries, key_rows, value_rows, head_size, allowed):
    maxima, totals, running = state
    head_count = queries.shape[1] // head_size
    query_heads = queries.reshape(queries.shape[0], head_count, head_size)
    key_heads = key_rows.reshape(key_rows.shape[0], head_count, head_size)
    value_heads = value_rows.reshape(value_rows.shape[0], head_count, head_size)
    scores = jnp.einsum(
        "qhd,khd->hqk", query_heads, key_heads, preferred_element_type=jnp.float32
    ) * (1.0 / math.sqrt(head_size))
    if allowed is not None:
        scores = jnp.where(allowed[None, None, :], scores, -1e30)
    new_peak = jnp.maximum(maxima, jnp.max(scores, axis=2))
    weights = jnp.exp(scores - new_peak[:, :, None])
    if allowed is not None:
        weights = jnp.where(allowed[None, None, :], weights, 0.0)
    rescale = jnp.exp(maxima - new_peak)
    totals = totals * rescale + jnp.sum(weights, axis=2)
    running = running * rescale[:, :, None] + jnp.einsum(
        "hqk,khd->hqd",
        weights.astype(jnp.bfloat16),
        value_heads,
        preferred_element_type=jnp.float32,
    )
    return (new_peak, totals, running)


def finish(state, head_size):
    _, totals, running = state
    result = running / totals[:, :, None]
    return (
        result.transpose(1, 0, 2)
        .reshape(result.shape[1], result.shape[0] * head_size)
        .astype(jnp.bfloat16)
    )


def permitted(key_blocks, position, table_row, wide_count):
    offsets = key_blocks - position + REACH
    matches = (offsets[:, None] == jnp.arange(2 * REACH + 1, dtype=jnp.int32)[None, :]) & (
        table_row[None, :] > 0
    )
    inside = (key_blocks >= 0) & (key_blocks < wide_count)
    return jnp.any(matches, axis=1) & inside


def shards(
    video_hidden,
    audio_hidden,
    video_query,
    video_key,
    video_value,
    audio_query,
    audio_key,
    audio_value,
    cross_video_query,
    cross_audio_key,
    cross_audio_value,
    cross_audio_query,
    cross_video_key,
    cross_video_value,
    video_self_out,
    video_cross_out,
    audio_self_out,
    audio_cross_out,
    intersection,
):
    position = lax.axis_index("wide")
    wide_count = lax.axis_size("wide")
    video_count = video_query.shape[0]
    audio_count = audio_query.shape[0]
    head_count = video_query.shape[1] // HDV
    video_start = empty_state(video_count, head_count, HDV)
    audio_start = empty_state(audio_count, head_count, HDA)
    carried = (video_start, audio_start)
    portion = (
        lax.all_gather(video_key, "wide", axis=0, tiled=True),
        lax.all_gather(video_value, "wide", axis=0, tiled=True),
        lax.all_gather(audio_key, "wide", axis=0, tiled=True),
        lax.all_gather(audio_value, "wide", axis=0, tiled=True),
    )
    video_state = absorb(carried[0], video_query, portion[0], portion[1], HDV, None)
    audio_state = absorb(carried[1], audio_query, portion[2], portion[3], HDA, None)
    table_row = lax.dynamic_slice_in_dim(intersection, position, 1, 0)[0]
    padded_table = jnp.pad(intersection, ((REACH, REACH), (0, 0)))
    flag_row = jnp.diagonal(
        jnp.fliplr(lax.dynamic_slice_in_dim(padded_table, position, 2 * REACH + 1, 0))
    )
    stacked = jnp.concatenate(
        [cross_audio_key, cross_audio_value, cross_video_key, cross_video_value], 0
    )

    def take_cross(carried, portion, block):
        audio_keys = portion[:audio_count]
        audio_values = portion[audio_count : 2 * audio_count]
        video_keys = portion[2 * audio_count : 2 * audio_count + video_count]
        video_values = portion[2 * audio_count + video_count :]
        audio_blocks = jnp.full((audio_count,), block, jnp.int32)
        video_blocks = jnp.full((video_count,), block, jnp.int32)
        return (
            absorb(
                carried[0],
                cross_video_query,
                audio_keys,
                audio_values,
                HDA,
                permitted(audio_blocks, position, table_row, wide_count),
            ),
            absorb(
                carried[1],
                cross_audio_query,
                video_keys,
                video_values,
                HDA,
                permitted(video_blocks, position, flag_row, wide_count),
            ),
        )

    cross_start = (
        empty_state(video_count, head_count, HDA),
        empty_state(audio_count, head_count, HDA),
    )
    carried = take_cross(cross_start, stacked, position)
    for offset in range(-REACH, REACH + 1):
        if offset != 0:
            nearby = passed_along(stacked, "wide", -offset)
            carried = take_cross(carried, nearby, position + offset)
    to_video, to_audio = carried
    video_joined = jnp.concatenate([finish(video_state, HDV), finish(to_video, HDA)], 1)
    audio_joined = jnp.concatenate([finish(audio_state, HDA), finish(to_audio, HDA)], 1)
    video_weights = jnp.concatenate([video_self_out, video_cross_out], 0)
    audio_weights = jnp.concatenate([audio_self_out, audio_cross_out], 0)
    video_terms = jnp.dot(
        video_joined,
        lax.all_gather(video_weights, "wide", axis=1, tiled=True),
        preferred_element_type=jnp.float32,
    )
    audio_terms = jnp.dot(
        audio_joined,
        lax.all_gather(audio_weights, "wide", axis=1, tiled=True),
        preferred_element_type=jnp.float32,
    )
    video_sum, audio_sum = (
        lax.psum_scatter(
            video_terms.astype(jnp.bfloat16), "heads", scatter_dimension=1, tiled=True
        ).astype(jnp.float32),
        lax.psum_scatter(
            audio_terms.astype(jnp.bfloat16), "heads", scatter_dimension=1, tiled=True
        ).astype(jnp.float32),
    )
    video_out = (video_hidden.astype(jnp.float32) + video_sum).astype(jnp.bfloat16)
    audio_out = (audio_hidden.astype(jnp.float32) + audio_sum).astype(jnp.bfloat16)
    return (video_out, audio_out)


VMEM = pl.BlockSpec(memory_space=pltpu.VMEM)
SMEM = pl.BlockSpec(memory_space=pltpu.SMEM)
HBM = pl.BlockSpec(memory_space=pltpu.HBM)
KERNEL_BYTES = 24 * 1024 * 1024


def kernel_call(kernel, scalars, arrays, out_shapes, scratch=(), spaces=None, final=False, held_as=jnp.bfloat16):
    spaces = spaces or [pltpu.VMEM] * len(arrays)
    specs = {pltpu.VMEM: VMEM, pltpu.HBM: HBM}
    out_space = pltpu.HBM if final else pltpu.VMEM
    call = pl.pallas_call(
        kernel,
        in_specs=[SMEM] * len(scalars)
        + [VMEM if s is None else specs[s] for s in spaces],
        out_specs=[VMEM] * len(out_shapes),
        out_shape=[out_space(s, held_as) for s in out_shapes],
        scratch_shapes=list(scratch),
        compiler_params=pltpu.CompilerParams(vmem_limit_bytes=KERNEL_BYTES),
    )
    arrays = [
        pltpu.with_memory_space_constraint(a, pltpu.HBM if s is None else s)
        for a, s in zip(arrays, spaces)
    ]
    return call(*scalars, *arrays)


def flip(tile):
    return jnp.concatenate([tile[:, HDA:], tile[:, :HDA]], axis=1)


def pack_wide_kernel(place_ref, *refs):
    sems = refs[-1]
    sources, outs = refs[:3], refs[3:-1]
    count = len(outs)
    rows = sources[0].shape[0]
    copies = []
    for shift in range(count):
        head = jnp.bitwise_xor(place_ref[0], shift)
        lanes = pl.ds(pl.multiple_of(head * HDV, HDV), HDV)
        for i, source in enumerate(sources):
            copies.append(
                pltpu.make_async_copy(
                    source.at[:, lanes],
                    outs[shift].at[pl.ds(i * rows, rows), :],
                    sems.at[shift * len(sources) + i],
                )
            )
    for copy in copies:
        copy.start()
    for copy in copies:
        copy.wait()


def pack_narrow_kernel(place_ref, aq, ak, av, cvq, cak, cav, caq, cvk, cvv, *outs):
    count = len(outs)
    video_count = cvq.shape[0]
    audio_count = aq.shape[0]
    half = video_count // 2
    for shift in range(count):
        head = jnp.bitwise_xor(place_ref[0], shift)
        lanes = pl.ds(pl.multiple_of((head // 2) * HDV, HDV), HDV)
        odd = lax.rem(head, 2) == 1
        out = outs[shift]
        lane = lax.broadcasted_iota(jnp.int32, (1, HDV), 1)

        def put(row, left, right):
            left, right = left.astype(jnp.float32), right.astype(jnp.float32)
            left = jnp.where(odd, flip(left), left)
            right = jnp.where(odd, right, flip(right))
            out[row : row + left.shape[0], :] = jnp.where(lane < HDA, left, right).astype(
                jnp.bfloat16
            )

        row = 0
        put(row, cvq[:, lanes], cvk[:, lanes])
        row += video_count
        put(row, cvv[:half, lanes], cvv[half:, lanes])
        row += half
        for left, right in ((aq, ak), (av, caq), (cak, cav)):
            put(row, left[:, lanes], right[:, lanes])
            row += audio_count


def softmax_mix(scores, values):
    peak = jnp.max(scores, axis=1, keepdims=True)
    weights = jnp.exp(scores - peak)
    totals = jnp.sum(weights, axis=1, keepdims=True)
    mixed = jnp.dot(
        weights.astype(jnp.bfloat16), values, preferred_element_type=jnp.float32
    )
    return mixed / totals


def dot_t(left, right):
    return lax.dot_general(
        left, right, (((1,), (1,)), ((), ())), preferred_element_type=jnp.float32
    )


def attend_wide_kernel(place_ref, head_ref, *refs):
    parts, outs, sorted_rows = refs[:-3], refs[-3:-1], refs[-1]
    count = len(parts)
    rows = parts[0].shape[0] // 3
    side = rows // (2 * CHUNKS)
    keys = jnp.concatenate([p[rows : 2 * rows, :] for p in parts], axis=0)
    values = jnp.concatenate([p[2 * rows :, :] for p in parts], axis=0)
    scale = 1.0 / math.sqrt(HDV)
    for shift in range(count):
        block = jnp.bitwise_xor(place_ref[0], shift)
        scores = dot_t(parts[shift][:rows, :], keys) * scale
        mixed = softmax_mix(scores, values).astype(jnp.bfloat16)
        for half in range(2):
            far, near = owner_of(block, half, head_ref[0], count)
            for c in range(CHUNKS):
                row = (2 * c + half) * side
                sorted_rows[far, c, near, half] = mixed[row : row + side]
    for far in range(2):
        outs[far][...] = sorted_rows[far].reshape(outs[far].shape)


def owner_of(block, half, head_place, count):
    owner = jnp.bitwise_xor(block, half * (count // 2))
    apart = jnp.bitwise_xor(owner, head_place)
    return apart // 2, lax.rem(apart, 2)


def attend_narrow_kernel(video_count, audio_count, place_ref, head_ref, table_ref, *refs):
    parts, outs, (sorted_video, sorted_audio) = refs[:-4], refs[-4:-2], refs[-2:]
    count = len(parts)
    blocks = [jnp.bitwise_xor(place_ref[0], shift) for shift in range(count)]
    half = video_count // 2
    r_value = video_count
    r_audio = r_value + half

    def flag(video_block, audio_block):
        offset = audio_block - video_block + REACH
        inside = (offset >= 0) & (offset <= 2 * REACH)
        entry = table_ref[video_block, jnp.clip(offset, 0, 2 * REACH)]
        return (inside & (entry > 0)).astype(jnp.int32)

    flags = [[flag(b, a) for a in blocks] for b in blocks]

    def masked(scores, row_flags, width):
        block = lax.broadcasted_iota(jnp.int32, (1, scores.shape[1]), 1) // width
        keep = jnp.zeros((1, scores.shape[1]), jnp.int32)
        for i, value in enumerate(row_flags):
            keep = jnp.where(block == i, value, keep)
        return jnp.where(keep > 0, scores, -1e30)

    def rows(start, size):
        return jnp.concatenate([p[start : start + size, :] for p in parts], axis=0)

    first = rows(r_audio, audio_count)
    second = rows(r_audio + audio_count, audio_count)
    third = rows(r_audio + 2 * audio_count, audio_count)
    scale = 1.0 / math.sqrt(HDA)
    cross_audio_key, cross_audio_value = third[:, :HDA], third[:, HDA:]
    side = video_count // (2 * CHUNKS)
    small = audio_count // 2
    for i in range(count):
        scores = dot_t(parts[i][:video_count, :HDA], cross_audio_key) * scale
        mixed = softmax_mix(masked(scores, flags[i], audio_count), cross_audio_value)
        for half in range(2):
            far, near = owner_of(blocks[i], half, head_ref[0], count)
            for c in range(CHUNKS):
                row = (2 * c + half) * side
                sorted_video[far, c, near, :, half * HDA : (half + 1) * HDA] = mixed[
                    row : row + side
                ]
    audio_self = softmax_mix(
        dot_t(first[:, :HDA], first[:, HDA:]) * scale, second[:, :HDA]
    )
    queries = second[:, HDA:]
    keys = jnp.concatenate([p[:video_count, HDA:] for p in parts], axis=0)
    values = jnp.concatenate(
        [
            rows_of
            for p in parts
            for rows_of in (p[r_value:r_audio, :HDA], p[r_value:r_audio, HDA:])
        ],
        axis=0,
    )
    for i in range(count):
        lo, hi = i * audio_count, (i + 1) * audio_count
        scores = dot_t(queries[lo:hi], keys) * scale
        mixed = softmax_mix(
            masked(scores, [flags[j][i] for j in range(count)], video_count), values
        )
        both = jnp.concatenate([audio_self[lo:hi], mixed], axis=1)
        for half in range(2):
            far, near = owner_of(blocks[i], half, head_ref[0], count)
            sorted_audio[far, near, half] = both[half * small : (half + 1) * small]
    video_rows = 2 * CHUNKS * side
    for far in range(2):
        outs[far][:video_rows, :] = (
            sorted_video[far].reshape(video_rows, HDV).astype(jnp.bfloat16)
        )
        outs[far][video_rows:, :] = (
            sorted_audio[far].reshape(4 * small, HDV).astype(jnp.bfloat16)
        )


def join_kernel(first, second, out):
    rows = first.shape[0]
    out[:rows, :] = first[...]
    out[rows:, :] = second[...]


def order_kernel(place_ref, vs_w, vc_w, as_w, ac_w, first_w, second_w, cross_w, audio_w):
    count = vs_w.shape[0] // HDV
    for shift in range(count):
        head = jnp.bitwise_xor(place_ref[0], shift)
        wide = pl.ds(pl.multiple_of(head * HDV, HDV), HDV)
        small = pl.ds(pl.multiple_of(head * HDA, HDA), HDA)
        at = (shift % (count // 2)) * HDV
        (first_w, second_w)[shift // (count // 2)][at : at + HDV, :] = vs_w[wide, :]
        cross_w[shift * HDA : (shift + 1) * HDA, :] = vc_w[small, :]
        audio_w[shift * HDV : shift * HDV + HDA, :] = as_w[small, :]
        audio_w[shift * HDV + HDA : (shift + 1) * HDV, :] = ac_w[small, :]


def project_wide_kernel(own_first, own_second, far_first, far_second, *refs):
    slots, out = refs[:-1], refs[-1]
    rows = slots[0].shape[0] // 2
    total = 0.0
    for far, pair in enumerate(((own_first, own_second), (far_first, far_second))):
        found = [slot[far * rows : (far + 1) * rows, :] for slot in slots]
        for i, weights in enumerate(pair):
            wide = jnp.concatenate(found[2 * i : 2 * i + 2], axis=1)
            total = total + jnp.dot(
                wide, weights[...], preferred_element_type=jnp.float32
            )
    out[...] = total


def project_narrow_kernel(own_w, far_w, own_audio_w, far_audio_w, begun, *refs):
    slots, outs = refs[:-2], refs[-2:]
    count = len(slots)
    width = own_audio_w.shape[1]
    folds = own_w.shape[1] // width
    side = begun.shape[0] // (4 * CHUNKS)
    video_rows = 2 * CHUNKS * side
    rows = slots[0].shape[0] // 2
    small = (rows - video_rows) // 4
    lane = lax.broadcasted_iota(jnp.int32, (1, HDV), 1)
    total = begun[...]
    audio_total = 0.0
    for far in range(2):
        weights, audio_weights = ((own_w, own_audio_w), (far_w, far_audio_w))[far]
        found = [
            slot[far * rows : far * rows + video_rows, :].astype(jnp.float32)
            for slot in slots
        ]
        flipped = [flip(t) for t in found]
        halves = [
            jnp.concatenate(
                [
                    jnp.where(
                        lane < HDA,
                        (flipped if half else found)[pair],
                        (found if half else flipped)[pair + 1],
                    ).astype(jnp.bfloat16)
                    for pair in range(0, count, 2)
                ],
                axis=1,
            )
            for half in range(2)
        ]
        lines = [
            halves[half][i * side : (i + 1) * side]
            for i in range(2 * CHUNKS)
            for half in range(2)
        ]
        total = total + jnp.dot(
            jnp.concatenate(lines, axis=0),
            weights[...],
            preferred_element_type=jnp.float32,
        )
        found = [slot[far * rows + video_rows : (far + 1) * rows, :] for slot in slots]
        audio_total = audio_total + jnp.dot(
            jnp.concatenate(found, axis=1), audio_weights[...], preferred_element_type=jnp.float32
        )
    total = total.astype(jnp.bfloat16)
    audio_total = audio_total.astype(jnp.bfloat16)
    for near in range(2):
        for half in range(2):
            for c in range(CHUNKS):
                row = ((2 * c + near) * 2 + half) * side
                for fold in range(folds):
                    at = (c * folds + fold) * side
                    outs[near][half, at : at + side, :] = total[
                        row : row + side, fold * width : (fold + 1) * width
                    ]
            row = (near * 2 + half) * small
            outs[near][half, CHUNKS * folds * side :, :] = audio_total[row : row + small]


def settle_kernel(kept, arrived, *outs):
    for half in range(2):
        total = kept[half].astype(jnp.float32) + arrived[half].astype(jnp.float32)
        outs[half][...] = total.astype(jnp.bfloat16)


def finish_kernel(video_hidden, audio_hidden, *refs):
    parts, (video_out, audio_out) = refs[:-2], refs[-2:]
    side = video_hidden.shape[0] // (2 * CHUNKS)
    small = audio_hidden.shape[0] // 2
    width = audio_hidden.shape[1]
    folds = video_hidden.shape[1] // width
    for half, part in enumerate(parts):
        for c in range(CHUNKS):
            row = (2 * c + half) * side
            rows = slice(row, row + side)
            for fold in range(folds):
                lanes = slice(fold * width, (fold + 1) * width)
                at = (c * folds + fold) * side
                video_out[rows, lanes] = (
                    video_hidden[rows, lanes].astype(jnp.float32)
                    + part[at : at + side, :].astype(jnp.float32)
                ).astype(jnp.bfloat16)
        rows = slice(half * small, (half + 1) * small)
        audio_out[rows, :] = (
            audio_hidden[rows, :].astype(jnp.float32)
            + part[CHUNKS * folds * side :, :].astype(jnp.float32)
        ).astype(jnp.bfloat16)


CHUNKS = 1


def exchanged(pieces):
    count = len(pieces)
    return [pieces[0]] + [
        lax.ppermute(pieces[s], "wide", [(i, i ^ s) for i in range(count)])
        for s in range(1, count)
    ]


def shared_along(value):
    count = lax.axis_size("wide")
    found = {0: value}
    bit = count // 2
    while bit:
        pairs = [(i, i ^ bit) for i in range(count)]
        for seen in sorted(found):
            found[bit | seen] = lax.ppermute(found[seen], "wide", pairs)
        bit //= 2
    return [found[s] for s in range(count)]


def regrouped(
    video_hidden,
    audio_hidden,
    video_query,
    video_key,
    video_value,
    audio_query,
    audio_key,
    audio_value,
    cross_video_query,
    cross_audio_key,
    cross_audio_value,
    cross_audio_query,
    cross_video_key,
    cross_video_value,
    video_self_out,
    video_cross_out,
    audio_self_out,
    audio_cross_out,
    intersection,
):
    count = lax.axis_size("wide")
    place = lax.axis_index("wide").astype(jnp.int32).reshape(1)
    head_place = lax.axis_index("heads").astype(jnp.int32).reshape(1)
    video_count = video_query.shape[0]
    audio_count = audio_query.shape[0]
    wide = kernel_call(
        pack_wide_kernel,
        (place,),
        (video_query, video_key, video_value),
        [(3 * video_count, HDV)] * count,
        (pltpu.SemaphoreType.DMA((3 * count,)),),
        [pltpu.HBM] * 3,
    )
    wide = exchanged(wide)
    narrow = kernel_call(
        pack_narrow_kernel,
        (place,),
        (
            audio_query,
            audio_key,
            audio_value,
            cross_video_query,
            cross_audio_key,
            cross_audio_value,
            cross_audio_query,
            cross_video_key,
            cross_video_value,
        ),
        [(video_count + video_count // 2 + 3 * audio_count, HDV)] * count,
        spaces=[None] * 9,
    )
    narrow = exchanged(narrow)
    width = audio_self_out.shape[1]
    folds = video_self_out.shape[1] // width

    def across(value, bit):
        return lax.ppermute(value, "heads", [(i, i ^ bit) for i in range(count)])

    half_rows = count // 2 * HDV
    weights = kernel_call(
        order_kernel,
        (place,),
        (video_self_out, video_cross_out, audio_self_out, audio_cross_out),
        [(half_rows, folds * width)] * 2
        + [(count * HDA, folds * width), (count * 2 * HDA, width)],
        spaces=[None] * 4,
    )
    far_weights = [across(value, 2) for value in weights]
    side = video_count // (2 * CHUNKS)
    mine = count * video_count // 2
    near, far = kernel_call(
        attend_wide_kernel,
        (place, head_place),
        wide,
        [(mine, HDV)] * 2,
        (pltpu.VMEM((2, CHUNKS, 2, 2, side, HDV), jnp.bfloat16),),
    )
    far = across(far, 2)
    (message,) = kernel_call(join_kernel, (), (near, far), [(2 * mine, HDV)])
    wide_slots = shared_along(message)
    small = audio_count // 2
    rows = 2 * CHUNKS * side + 4 * small
    near, far = kernel_call(
        functools.partial(attend_narrow_kernel, video_count, audio_count),
        (place, head_place, intersection),
        narrow,
        [(rows, HDV)] * 2,
        (
            pltpu.VMEM((2, CHUNKS, 2, side, HDV), jnp.float32),
            pltpu.VMEM((2, 2, 2, small, HDV), jnp.float32),
        ),
    )
    far = across(far, 2)
    (message,) = kernel_call(join_kernel, (), (near, far), [(2 * rows, HDV)])
    narrow_slots = exchanged([message] * count)
    (begun,) = kernel_call(
        project_wide_kernel,
        (),
        (*weights[:2], *far_weights[:2], *wide_slots),
        [(mine, folds * width)],
        held_as=jnp.float32,
    )
    height = (video_count * folds + audio_count) // 2
    kept, leaving = kernel_call(
        project_narrow_kernel,
        (),
        (weights[2], far_weights[2], weights[3], far_weights[3], begun, *narrow_slots),
        [(2, height, width)] * 2,
    )
    halves = kernel_call(
        settle_kernel, (), (kept, across(leaving, 1)), [(height, width)] * 2
    )
    landed = [
        lax.ppermute(
            halves[half],
            ("wide", "heads"),
            [
                (w * count + h, (h ^ (half * (count // 2))) * count + w)
                for w in range(count)
                for h in range(count)
            ],
        )
        for half in range(2)
    ]
    return tuple(
        kernel_call(
            finish_kernel,
            (),
            (video_hidden, audio_hidden, *landed),
            [video_hidden.shape, audio_hidden.shape],
            final=True,
        )
    )


def dispatch(*operands):
    count = lax.axis_size("wide")
    head_count = operands[2].shape[1] // HDV
    whole = head_count == count == lax.axis_size("heads")
    if whole and count == 4 and operands[5].shape[0] % (16 * count) == 0:
        return regrouped(*operands)
    return shards(*operands)


def solution(mesh):
    placed = (
        P(("groups", "wide"), "heads"),
        P(("groups", "wide"), "heads"),
        P(("groups", "wide"), "heads"),
        P(("groups", "wide"), "heads"),
        P(("groups", "wide"), "heads"),
        P(("groups", "wide"), "heads"),
        P(("groups", "wide"), "heads"),
        P(("groups", "wide"), "heads"),
        P(("groups", "wide"), "heads"),
        P(("groups", "wide"), "heads"),
        P(("groups", "wide"), "heads"),
        P(("groups", "wide"), "heads"),
        P(("groups", "wide"), "heads"),
        P(("groups", "wide"), "heads"),
        P("heads", "wide"),
        P("heads", "wide"),
        P("heads", "wide"),
        P("heads", "wide"),
        P("groups", None),
    )
    return jax.shard_map(
        dispatch,
        mesh=mesh,
        in_specs=placed,
        out_specs=(P(("groups", "wide"), "heads"), P(("groups", "wide"), "heads")),
        check_vma=False,
    )
```

```python
import functools
import math

import jax
import jax.numpy as jnp
from jax import lax
from jax.experimental import pallas as pl
from jax.experimental.pallas import tpu as pltpu
from jax.sharding import PartitionSpec as P

HDV = 128
HDA = 64
REACH = 2


def passed_along(value, axis, by):
    length = lax.axis_size(axis)
    pairs = [(i, i + by) for i in range(length) if 0 <= i + by < length]
    return lax.ppermute(value, axis, pairs)


def empty_state(row_count, head_count, head_size):
    return (
        jnp.full((head_count, row_count), -1e30, jnp.float32),
        jnp.zeros((head_count, row_count), jnp.float32),
        jnp.zeros((head_count, row_count, head_size), jnp.float32),
    )


def absorb(state, queries, key_rows, value_rows, head_size, allowed):
    maxima, totals, running = state
    head_count = queries.shape[1] // head_size
    query_heads = queries.reshape(queries.shape[0], head_count, head_size)
    key_heads = key_rows.reshape(key_rows.shape[0], head_count, head_size)
    value_heads = value_rows.reshape(value_rows.shape[0], head_count, head_size)
    scores = jnp.einsum(
        "qhd,khd->hqk", query_heads, key_heads, preferred_element_type=jnp.float32
    ) * (1.0 / math.sqrt(head_size))
    if allowed is not None:
        scores = jnp.where(allowed[None, None, :], scores, -1e30)
    new_peak = jnp.maximum(maxima, jnp.max(scores, axis=2))
    weights = jnp.exp(scores - new_peak[:, :, None])
    if allowed is not None:
        weights = jnp.where(allowed[None, None, :], weights, 0.0)
    rescale = jnp.exp(maxima - new_peak)
    totals = totals * rescale + jnp.sum(weights, axis=2)
    running = running * rescale[:, :, None] + jnp.einsum(
        "hqk,khd->hqd",
        weights.astype(jnp.bfloat16),
        value_heads,
        preferred_element_type=jnp.float32,
    )
    return (new_peak, totals, running)


def finish(state, head_size):
    _, totals, running = state
    result = running / totals[:, :, None]
    return (
        result.transpose(1, 0, 2)
        .reshape(result.shape[1], result.shape[0] * head_size)
        .astype(jnp.bfloat16)
    )


def permitted(key_blocks, position, table_row, wide_count):
    offsets = key_blocks - position + REACH
    matches = (offsets[:, None] == jnp.arange(2 * REACH + 1, dtype=jnp.int32)[None, :]) & (
        table_row[None, :] > 0
    )
    inside = (key_blocks >= 0) & (key_blocks < wide_count)
    return jnp.any(matches, axis=1) & inside


def shards(
    video_hidden,
    audio_hidden,
    video_query,
    video_key,
    video_value,
    audio_query,
    audio_key,
    audio_value,
    cross_video_query,
    cross_audio_key,
    cross_audio_value,
    cross_audio_query,
    cross_video_key,
    cross_video_value,
    video_self_out,
    video_cross_out,
    audio_self_out,
    audio_cross_out,
    intersection,
):
    position = lax.axis_index("wide")
    wide_count = lax.axis_size("wide")
    video_count = video_query.shape[0]
    audio_count = audio_query.shape[0]
    head_count = video_query.shape[1] // HDV
    video_start = empty_state(video_count, head_count, HDV)
    audio_start = empty_state(audio_count, head_count, HDA)
    carried = (video_start, audio_start)
    portion = (
        lax.all_gather(video_key, "wide", axis=0, tiled=True),
        lax.all_gather(video_value, "wide", axis=0, tiled=True),
        lax.all_gather(audio_key, "wide", axis=0, tiled=True),
        lax.all_gather(audio_value, "wide", axis=0, tiled=True),
    )
    video_state = absorb(carried[0], video_query, portion[0], portion[1], HDV, None)
    audio_state = absorb(carried[1], audio_query, portion[2], portion[3], HDA, None)
    table_row = lax.dynamic_slice_in_dim(intersection, position, 1, 0)[0]
    padded_table = jnp.pad(intersection, ((REACH, REACH), (0, 0)))
    flag_row = jnp.diagonal(
        jnp.fliplr(lax.dynamic_slice_in_dim(padded_table, position, 2 * REACH + 1, 0))
    )
    stacked = jnp.concatenate(
        [cross_audio_key, cross_audio_value, cross_video_key, cross_video_value], 0
    )

    def take_cross(carried, portion, block):
        audio_keys = portion[:audio_count]
        audio_values = portion[audio_count : 2 * audio_count]
        video_keys = portion[2 * audio_count : 2 * audio_count + video_count]
        video_values = portion[2 * audio_count + video_count :]
        audio_blocks = jnp.full((audio_count,), block, jnp.int32)
        video_blocks = jnp.full((video_count,), block, jnp.int32)
        return (
            absorb(
                carried[0],
                cross_video_query,
                audio_keys,
                audio_values,
                HDA,
                permitted(audio_blocks, position, table_row, wide_count),
            ),
            absorb(
                carried[1],
                cross_audio_query,
                video_keys,
                video_values,
                HDA,
                permitted(video_blocks, position, flag_row, wide_count),
            ),
        )

    cross_start = (
        empty_state(video_count, head_count, HDA),
        empty_state(audio_count, head_count, HDA),
    )
    carried = take_cross(cross_start, stacked, position)
    for offset in range(-REACH, REACH + 1):
        if offset != 0:
            nearby = passed_along(stacked, "wide", -offset)
            carried = take_cross(carried, nearby, position + offset)
    to_video, to_audio = carried
    video_joined = jnp.concatenate([finish(video_state, HDV), finish(to_video, HDA)], 1)
    audio_joined = jnp.concatenate([finish(audio_state, HDA), finish(to_audio, HDA)], 1)
    video_weights = jnp.concatenate([video_self_out, video_cross_out], 0)
    audio_weights = jnp.concatenate([audio_self_out, audio_cross_out], 0)
    video_terms = jnp.dot(
        video_joined,
        lax.all_gather(video_weights, "wide", axis=1, tiled=True),
        preferred_element_type=jnp.float32,
    )
    audio_terms = jnp.dot(
        audio_joined,
        lax.all_gather(audio_weights, "wide", axis=1, tiled=True),
        preferred_element_type=jnp.float32,
    )
    video_sum, audio_sum = (
        lax.psum_scatter(
            video_terms.astype(jnp.bfloat16), "heads", scatter_dimension=1, tiled=True
        ).astype(jnp.float32),
        lax.psum_scatter(
            audio_terms.astype(jnp.bfloat16), "heads", scatter_dimension=1, tiled=True
        ).astype(jnp.float32),
    )
    video_out = (video_hidden.astype(jnp.float32) + video_sum).astype(jnp.bfloat16)
    audio_out = (audio_hidden.astype(jnp.float32) + audio_sum).astype(jnp.bfloat16)
    return (video_out, audio_out)


VMEM = pl.BlockSpec(memory_space=pltpu.VMEM)
SMEM = pl.BlockSpec(memory_space=pltpu.SMEM)
HBM = pl.BlockSpec(memory_space=pltpu.HBM)
KERNEL_BYTES = 24 * 1024 * 1024


def kernel_call(kernel, scalars, arrays, out_shapes, scratch=(), spaces=None, final=False, held_as=jnp.bfloat16):
    spaces = spaces or [pltpu.VMEM] * len(arrays)
    specs = {pltpu.VMEM: VMEM, pltpu.HBM: HBM}
    out_space = pltpu.HBM if final else pltpu.VMEM
    call = pl.pallas_call(
        kernel,
        in_specs=[SMEM] * len(scalars)
        + [VMEM if s is None else specs[s] for s in spaces],
        out_specs=[VMEM] * len(out_shapes),
        out_shape=[out_space(s, held_as) for s in out_shapes],
        scratch_shapes=list(scratch),
        compiler_params=pltpu.CompilerParams(vmem_limit_bytes=KERNEL_BYTES),
    )
    arrays = [
        pltpu.with_memory_space_constraint(a, pltpu.HBM if s is None else s)
        for a, s in zip(arrays, spaces)
    ]
    return call(*scalars, *arrays)


def flip(tile):
    return jnp.concatenate([tile[:, HDA:], tile[:, :HDA]], axis=1)


def pack_wide_kernel(first_shift, place_ref, *refs):
    sems = refs[-1]
    sources, outs = refs[:3], refs[3:-1]
    rows = sources[0].shape[0]
    copies = []
    for shift in range(len(outs)):
        head = jnp.bitwise_xor(place_ref[0], first_shift + shift)
        lanes = pl.ds(pl.multiple_of(head * HDV, HDV), HDV)
        for i, source in enumerate(sources):
            copies.append(
                pltpu.make_async_copy(
                    source.at[:, lanes],
                    outs[shift].at[pl.ds(i * rows, rows), :],
                    sems.at[shift * len(sources) + i],
                )
            )
    for copy in copies:
        copy.start()
    for copy in copies:
        copy.wait()


def pack_narrow_kernel(first_shift, place_ref, aq, ak, av, cvq, cak, cav, caq, cvk, cvv, *outs):
    video_count = cvq.shape[0]
    audio_count = aq.shape[0]
    half = video_count // 2
    for shift in range(len(outs)):
        head = jnp.bitwise_xor(place_ref[0], first_shift + shift)
        lanes = pl.ds(pl.multiple_of((head // 2) * HDV, HDV), HDV)
        odd = lax.rem(head, 2) == 1
        out = outs[shift]
        lane = lax.broadcasted_iota(jnp.int32, (1, HDV), 1)

        def put(row, left, right):
            left, right = left.astype(jnp.float32), right.astype(jnp.float32)
            left = jnp.where(odd, flip(left), left)
            right = jnp.where(odd, right, flip(right))
            out[row : row + left.shape[0], :] = jnp.where(lane < HDA, left, right).astype(
                jnp.bfloat16
            )

        row = 0
        put(row, cvq[:, lanes], cvk[:, lanes])
        row += video_count
        put(row, cvv[:half, lanes], cvv[half:, lanes])
        row += half
        for left, right in ((aq, ak), (av, caq), (cak, cav)):
            put(row, left[:, lanes], right[:, lanes])
            row += audio_count


def softmax_mix(scores, values):
    peak = jnp.max(scores, axis=1, keepdims=True)
    weights = jnp.exp2(scores - peak)
    totals = jnp.sum(weights, axis=1, keepdims=True)
    mixed = jnp.dot(
        weights.astype(jnp.bfloat16), values, preferred_element_type=jnp.float32
    )
    return mixed / totals


def dot_t(left, right):
    return lax.dot_general(
        left, right, (((1,), (1,)), ((), ())), preferred_element_type=jnp.float32
    )


def attend_wide_kernel(place_ref, head_ref, *refs):
    parts, outs, sorted_rows = refs[:-3], refs[-3:-1], refs[-1]
    count = len(parts)
    rows = parts[0].shape[0] // 3
    side = rows // (2 * CHUNKS)
    keys = jnp.concatenate([p[rows : 2 * rows, :] for p in parts], axis=0)
    values = jnp.concatenate([p[2 * rows :, :] for p in parts], axis=0)
    scale = math.log2(math.e) / math.sqrt(HDV)
    for shift in range(count):
        block = jnp.bitwise_xor(place_ref[0], shift)
        scores = dot_t(parts[shift][:rows, :], keys) * scale
        mixed = softmax_mix(scores, values).astype(jnp.bfloat16)
        for half in range(2):
            far, near = owner_of(block, half, head_ref[0], count)
            for c in range(CHUNKS):
                row = (2 * c + half) * side
                sorted_rows[far, c, near, half] = mixed[row : row + side]
    for far in range(2):
        outs[far][...] = sorted_rows[far].reshape(outs[far].shape)


def owner_of(block, half, head_place, count):
    owner = jnp.bitwise_xor(block, half * (count // 2))
    apart = jnp.bitwise_xor(owner, head_place)
    return apart // 2, lax.rem(apart, 2)


def attend_narrow_kernel(video_count, audio_count, place_ref, head_ref, table_ref, *refs):
    parts, outs, (sorted_video, sorted_audio) = refs[:-4], refs[-4:-2], refs[-2:]
    count = len(parts)
    blocks = [jnp.bitwise_xor(place_ref[0], shift) for shift in range(count)]
    half_rows = video_count // 2
    r_value = video_count
    r_audio = r_value + half_rows

    def flag(video_block, audio_block):
        offset = audio_block - video_block + REACH
        inside = (offset >= 0) & (offset <= 2 * REACH)
        entry = table_ref[video_block, jnp.clip(offset, 0, 2 * REACH)]
        return (inside & (entry > 0)).astype(jnp.int32)

    flags = [[flag(b, a) for a in blocks] for b in blocks]

    def masked(scores, row_flags, width):
        block = lax.broadcasted_iota(jnp.int32, (1, scores.shape[1]), 1) // width
        keep = jnp.zeros((1, scores.shape[1]), jnp.int32)
        for i, value in enumerate(row_flags):
            keep = jnp.where(block == i, value, keep)
        return jnp.where(keep > 0, scores, -1e30)

    def rows(start, size):
        return jnp.concatenate([p[start : start + size, :] for p in parts], axis=0)

    lane = lax.broadcasted_iota(jnp.int32, (1, HDV), 1)

    def left_only(tile):
        return jnp.where(lane < HDA, tile, jnp.zeros_like(tile))

    def right_only(tile):
        return jnp.where(lane < HDA, jnp.zeros_like(tile), tile)

    first = rows(r_audio, audio_count)
    second = rows(r_audio + audio_count, audio_count)
    third = rows(r_audio + 2 * audio_count, audio_count)
    scale = math.log2(math.e) / math.sqrt(HDA)
    cross_keys = left_only(third)
    cross_values = jnp.concatenate([third[:, HDA:], third[:, HDA:]], axis=1)
    side = video_count // (2 * CHUNKS)
    small = audio_count // 2
    keys = rows(0, video_count)
    scores = dot_t(keys, cross_keys) * scale
    mixed_video = softmax_mix(
        jnp.concatenate(
            [
                masked(scores[i * video_count : (i + 1) * video_count], flags[i], audio_count)
                for i in range(count)
            ],
            axis=0,
        ),
        cross_values,
    )
    for i in range(count):
        mixed = mixed_video[i * video_count : (i + 1) * video_count]
        for half in range(2):
            far, near = owner_of(blocks[i], half, head_ref[0], count)
            for c in range(CHUNKS):
                row = (2 * c + half) * side
                lanes = slice(half * HDA, (half + 1) * HDA)
                sorted_video[far, c, near, :, lanes] = mixed[row : row + side, lanes]
    audio_self = softmax_mix(dot_t(left_only(first), flip(first)) * scale, second)
    values = rows(r_value, half_rows)
    scores = dot_t(right_only(second), keys) * scale
    scores = jnp.concatenate(
        [
            masked(
                scores[i * audio_count : (i + 1) * audio_count],
                [flags[j][i] for j in range(count)],
                video_count,
            )
            for i in range(count)
        ],
        axis=0,
    )
    peak = jnp.max(scores, axis=1, keepdims=True)
    weights = jnp.exp2(scores - peak)
    totals = jnp.sum(weights, axis=1, keepdims=True)
    weights = weights.astype(jnp.bfloat16)
    low, high = (
        jnp.dot(
            jnp.concatenate(
                [
                    weights[:, at + k * half_rows : at + (k + 1) * half_rows]
                    for at in range(0, count * video_count, video_count)
                ],
                axis=1,
            ),
            values,
            preferred_element_type=jnp.float32,
        )
        for k in range(2)
    )
    audio_both = jnp.where(lane < HDA, audio_self, (flip(low) + high) / totals)
    for i in range(count):
        lo, hi = i * audio_count, (i + 1) * audio_count
        both = audio_both[lo:hi]
        for half in range(2):
            far, near = owner_of(blocks[i], half, head_ref[0], count)
            sorted_audio[far, near, half] = both[half * small : (half + 1) * small]
    block_rows = 2 * side
    for far in range(2):
        at = 0
        for c in range(CHUNKS):
            outs[far][at : at + block_rows, :] = (
                sorted_video[far, c].reshape(block_rows, HDV).astype(jnp.bfloat16)
            )
            at += block_rows
            if c == 0:
                outs[far][at : at + 4 * small, :] = (
                    sorted_audio[far].reshape(4 * small, HDV).astype(jnp.bfloat16)
                )
                at += 4 * small


def join_kernel(first, second, *outs):
    at = 0
    for out in outs:
        rows = out.shape[0] // 2
        out[:rows, :] = first[at : at + rows, :]
        out[rows:, :] = second[at : at + rows, :]
        at += rows


def order_kernel(place_ref, vs_w, vc_w, as_w, ac_w, first_w, second_w, cross_w, audio_w):
    count = vs_w.shape[0] // HDV
    for shift in range(count):
        head = jnp.bitwise_xor(place_ref[0], shift)
        wide = pl.ds(pl.multiple_of(head * HDV, HDV), HDV)
        small = pl.ds(pl.multiple_of(head * HDA, HDA), HDA)
        at = (shift % (count // 2)) * HDV
        (first_w, second_w)[shift // (count // 2)][at : at + HDV, :] = vs_w[wide, :]
        cross_w[shift * HDA : (shift + 1) * HDA, :] = vc_w[small, :]
        audio_w[shift * HDV : shift * HDV + HDA, :] = as_w[small, :]
        audio_w[shift * HDV + HDA : (shift + 1) * HDV, :] = ac_w[small, :]


def project_wide_kernel(own_first, own_second, far_first, far_second, *refs):
    slots, out = refs[:-1], refs[-1]
    rows = slots[0].shape[0] // 2
    total = 0.0
    for far, pair in enumerate(((own_first, own_second), (far_first, far_second))):
        found = [slot[far * rows : (far + 1) * rows, :] for slot in slots]
        for i, weights in enumerate(pair):
            wide = jnp.concatenate(found[2 * i : 2 * i + 2], axis=1)
            total = total + jnp.dot(
                wide, weights[...], preferred_element_type=jnp.float32
            )
    out[...] = total


def project_narrow_kernel(chunk, own_w, far_w, own_audio_w, far_audio_w, begun, *refs):
    slots, outs = refs[:-2], refs[-2:]
    count = len(slots)
    width = own_audio_w.shape[1]
    folds = own_w.shape[1] // width
    side = begun.shape[0] // (4 * CHUNKS)
    video_rows = 2 * side
    rows = slots[0].shape[0] // 2
    small = (rows - video_rows) // 4
    lane = lax.broadcasted_iota(jnp.int32, (1, HDV), 1)
    total = begun[chunk * 4 * side : (chunk + 1) * 4 * side, :]
    audio_total = 0.0
    for far in range(2):
        weights, audio_weights = ((own_w, own_audio_w), (far_w, far_audio_w))[far]
        found = [
            slot[far * rows : far * rows + video_rows, :].astype(jnp.float32)
            for slot in slots
        ]
        flipped = [flip(t) for t in found]
        halves = [
            jnp.concatenate(
                [
                    jnp.where(
                        lane < HDA,
                        (flipped if half else found)[pair],
                        (found if half else flipped)[pair + 1],
                    ).astype(jnp.bfloat16)
                    for pair in range(0, count, 2)
                ],
                axis=1,
            )
            for half in range(2)
        ]
        lines = [
            halves[half][i * side : (i + 1) * side]
            for i in range(2)
            for half in range(2)
        ]
        total = total + jnp.dot(
            jnp.concatenate(lines, axis=0),
            weights[...],
            preferred_element_type=jnp.float32,
        )
        if chunk == 0:
            found = [slot[far * rows + video_rows : (far + 1) * rows, :] for slot in slots]
            audio_total = audio_total + jnp.dot(
                jnp.concatenate(found, axis=1),
                audio_weights[...],
                preferred_element_type=jnp.float32,
            )
    total = total.astype(jnp.bfloat16)
    for near in range(2):
        for half in range(2):
            row = (near * 2 + half) * side
            for fold in range(folds):
                at = fold * side
                outs[near][half, at : at + side, :] = total[
                    row : row + side, fold * width : (fold + 1) * width
                ]
            if chunk == 0:
                row = (near * 2 + half) * small
                outs[near][half, folds * side :, :] = audio_total[row : row + small].astype(
                    jnp.bfloat16
                )


def settle_kernel(kept, arrived, *outs):
    for half in range(2):
        total = kept[half].astype(jnp.float32) + arrived[half].astype(jnp.float32)
        outs[half][...] = total.astype(jnp.bfloat16)


def finish_kernel(video_hidden, audio_hidden, *refs):
    parts, (video_out, audio_out) = refs[:-2], refs[-2:]
    side = video_hidden.shape[0] // (2 * CHUNKS)
    small = audio_hidden.shape[0] // 2
    width = audio_hidden.shape[1]
    folds = video_hidden.shape[1] // width
    for i, part in enumerate(parts):
        rows = slice(i * side, (i + 1) * side)
        for fold in range(folds):
            lanes = slice(fold * width, (fold + 1) * width)
            video_out[rows, lanes] = (
                video_hidden[rows, lanes].astype(jnp.float32)
                + part[fold * side : (fold + 1) * side, :].astype(jnp.float32)
            ).astype(jnp.bfloat16)
        if i < 2:
            rows = slice(i * small, (i + 1) * small)
            audio_out[rows, :] = (
                audio_hidden[rows, :].astype(jnp.float32)
                + part[folds * side :, :].astype(jnp.float32)
            ).astype(jnp.bfloat16)


CHUNKS = 2


def exchanged(pieces):
    count = len(pieces)
    return [pieces[0]] + [
        lax.ppermute(pieces[s], "wide", [(i, i ^ s) for i in range(count)])
        for s in range(1, count)
    ]


def shared_along(value):
    count = lax.axis_size("wide")
    found = {0: value}
    bit = count // 2
    while bit:
        pairs = [(i, i ^ bit) for i in range(count)]
        for seen in sorted(found):
            found[bit | seen] = lax.ppermute(found[seen], "wide", pairs)
        bit //= 2
    return [found[s] for s in range(count)]


def regrouped(
    video_hidden,
    audio_hidden,
    video_query,
    video_key,
    video_value,
    audio_query,
    audio_key,
    audio_value,
    cross_video_query,
    cross_audio_key,
    cross_audio_value,
    cross_audio_query,
    cross_video_key,
    cross_video_value,
    video_self_out,
    video_cross_out,
    audio_self_out,
    audio_cross_out,
    intersection,
):
    count = lax.axis_size("wide")
    place = lax.axis_index("wide").astype(jnp.int32).reshape(1)
    head_place = lax.axis_index("heads").astype(jnp.int32).reshape(1)
    video_count = video_query.shape[0]
    audio_count = audio_query.shape[0]
    wide = []
    for shifts in ((0, 1), (1, count)):
        wide += kernel_call(
            functools.partial(pack_wide_kernel, shifts[0]),
            (place,),
            (video_query, video_key, video_value),
            [(3 * video_count, HDV)] * (shifts[1] - shifts[0]),
            (pltpu.SemaphoreType.DMA((3 * (shifts[1] - shifts[0]),)),),
            [pltpu.HBM] * 3,
        )
    wide = exchanged(wide)
    narrow = []
    for shifts in ((0, 1), (1, count)):
        narrow += kernel_call(
            functools.partial(pack_narrow_kernel, shifts[0]),
            (place,),
            (
                audio_query,
                audio_key,
                audio_value,
                cross_video_query,
                cross_audio_key,
                cross_audio_value,
                cross_audio_query,
                cross_video_key,
                cross_video_value,
            ),
            [(video_count + video_count // 2 + 3 * audio_count, HDV)] * (shifts[1] - shifts[0]),
            spaces=[None] * 9,
        )
    narrow = exchanged(narrow)
    width = audio_self_out.shape[1]
    folds = video_self_out.shape[1] // width

    def across(value, bit):
        return lax.ppermute(value, "heads", [(i, i ^ bit) for i in range(count)])

    half_rows = count // 2 * HDV
    weights = kernel_call(
        order_kernel,
        (place,),
        (video_self_out, video_cross_out, audio_self_out, audio_cross_out),
        [(half_rows, folds * width)] * 2
        + [(count * HDA, folds * width), (count * 2 * HDA, width)],
        spaces=[None] * 4,
    )
    far_weights = [across(value, 2) for value in weights]
    side = video_count // (2 * CHUNKS)
    mine = count * video_count // 2
    near, far = kernel_call(
        attend_wide_kernel,
        (place, head_place),
        wide,
        [(mine, HDV)] * 2,
        (pltpu.VMEM((2, CHUNKS, 2, 2, side, HDV), jnp.bfloat16),),
    )
    far = across(far, 2)
    (message,) = kernel_call(join_kernel, (), (near, far), [(2 * mine, HDV)])
    wide_slots = shared_along(message)
    small = audio_count // 2
    rows = 2 * CHUNKS * side + 4 * small
    near, far = kernel_call(
        functools.partial(attend_narrow_kernel, video_count, audio_count),
        (place, head_place, intersection),
        narrow,
        [(rows, HDV)] * 2,
        (
            pltpu.VMEM((2, CHUNKS, 2, side, HDV), jnp.float32),
            pltpu.VMEM((2, 2, 2, small, HDV), jnp.float32),
        ),
    )
    far = across(far, 2)
    block_rows = 2 * side
    sizes = [block_rows + (4 * small if c == 0 else 0) for c in range(CHUNKS)]
    messages = kernel_call(
        join_kernel, (), (near, far), [(2 * size, HDV) for size in sizes]
    )
    narrow_slots = [exchanged([message] * count) for message in messages]
    (begun,) = kernel_call(
        project_wide_kernel,
        (),
        (*weights[:2], *far_weights[:2], *wide_slots),
        [(mine, folds * width)],
        held_as=jnp.float32,
    )
    landed = []
    for c in range(CHUNKS):
        height = side * folds + (small if c == 0 else 0)
        kept, leaving = kernel_call(
            functools.partial(project_narrow_kernel, c),
            (),
            (weights[2], far_weights[2], weights[3], far_weights[3], begun, *narrow_slots[c]),
            [(2, height, width)] * 2,
        )
        halves = kernel_call(
            settle_kernel, (), (kept, across(leaving, 1)), [(height, width)] * 2
        )
        landed += [
            lax.ppermute(
                halves[half],
                ("wide", "heads"),
                [
                    (w * count + h, (h ^ (half * (count // 2))) * count + w)
                    for w in range(count)
                    for h in range(count)
                ],
            )
            for half in range(2)
        ]
    return tuple(
        kernel_call(
            finish_kernel,
            (),
            (video_hidden, audio_hidden, *landed),
            [video_hidden.shape, audio_hidden.shape],
            final=True,
        )
    )


def dispatch(*operands):
    count = lax.axis_size("wide")
    head_count = operands[2].shape[1] // HDV
    whole = head_count == count == lax.axis_size("heads")
    if whole and count == 4 and operands[5].shape[0] % (16 * count) == 0:
        return regrouped(*operands)
    return shards(*operands)


def solution(mesh):
    placed = (
        P(("groups", "wide"), "heads"),
        P(("groups", "wide"), "heads"),
        P(("groups", "wide"), "heads"),
        P(("groups", "wide"), "heads"),
        P(("groups", "wide"), "heads"),
        P(("groups", "wide"), "heads"),
        P(("groups", "wide"), "heads"),
        P(("groups", "wide"), "heads"),
        P(("groups", "wide"), "heads"),
        P(("groups", "wide"), "heads"),
        P(("groups", "wide"), "heads"),
        P(("groups", "wide"), "heads"),
        P(("groups", "wide"), "heads"),
        P(("groups", "wide"), "heads"),
        P("heads", "wide"),
        P("heads", "wide"),
        P("heads", "wide"),
        P("heads", "wide"),
        P("groups", None),
    )
    return jax.shard_map(
        dispatch,
        mesh=mesh,
        in_specs=placed,
        out_specs=(P(("groups", "wide"), "heads"), P(("groups", "wide"), "heads")),
        check_vma=False,
    )
```
